32 devices in a mesh: group: 4 (over z), tensor: 2 (over y), role: 4 (over x, core).
Axes of the slice: x: 2, y: 2, z: 4, core: 2. Of those that a mesh axis runs over, the one named last changes fastest.
Arguments:
- tokens: bfloat16 [4, 1024, 2880], P('group', 'role'), may hold values from -6 to 6
- gain: float32 [2880], replicated, may hold values from 0.1 to 1.9
- q_weight: bfloat16 [2880, 2048], P(('group', 'role'), 'tensor'), may hold values from -0.109375 to 0.109375
- kv_weight: bfloat16 [2880, 512], P(('group', 'role'), 'tensor'), may hold values from -0.109375 to 0.109375
- out_weight: bfloat16 [2048, 2880], P('role', 'tensor'), may hold values from -0.5 to 0.5
- sinks: float32 [32], P('tensor'), may hold values from -1 to 3
- segments: int32 [4, 1024], P('group', 'role'), may hold values from 0 to 7, never falling along the last dimension, each value on 1 to 768 neighbouring positions
Outputs:
- mixed: bfloat16 [4, 1024, 2880], P('group', 'role', 'tensor')
The draws below stay inside these ranges and needn't reach their ends.
Inputs may be any that keep to these rules, and one draw needn't show every extreme that they name: `segments`: within a group, document numbers never fall along the positions; each document holds 1 to 768 positions and one holds exactly 768.
All inputs are finite; a program needn't handle non-finite values.
Results may differ from the reference program's by a relative error of at most 0.009.
Values may be sent and summed in bfloat16 or wider, within the bound.
No kernel may reach another device: no remote copies, remote signals or barrier semaphores. Data moves between devices by JAX's collectives and lax.ppermute only.
A program may use at most 64 MiB of HBM per device.

```python
import math
import jax
import jax.numpy as jnp
import numpy as np
from jax import lax

D = 2880
HEADS = 32
KV_HEADS = 4
HEAD_DIM = 64
TOK_DEV = 256
SEQ = 1024
DOCS = 8
DOC_MOST = 768
N_GROUP = 4


def steps_of(rng, shape, shards, smallest, top_value):
    factor_of = 1.0
    for position, blocks in shards:
        draws = jax.random.uniform(jax.random.fold_in(jax.random.fold_in(rng, 6), position), (blocks,), jnp.float32, smallest / len(shards), top_value / len(shards))
        factor_of = factor_of * jnp.repeat(jnp.exp(draws), shape[position] // blocks).reshape((-1,) + (1,) * (len(shape) - 1 - position))
    return factor_of


def length_profile(number_of, total, most, skew):
    portions = [(1 << 20) // math.isqrt(standing ** skew) + 1 for standing in range(2, number_of + 1)]
    surplus, given = total - most - (number_of - 1), [1] * (number_of - 1)
    while surplus > 0:
        candidates = [i for i in range(number_of - 1) if given[i] < most]
        pool, budget = sum([portions[i] for i in candidates]), surplus
        for i in candidates:
            more = min(most - given[i], max(1, budget * portions[i] // pool), surplus)
            given[i] = given[i] + more
            surplus = surplus - more
    return np.array([most] + given)


def ragged_sizes(key, count, total, reach, lean):
    if count == 2:
        one = jax.random.randint(key, (), max(1, total - reach), min(reach, total - 1) + 1)
        return jnp.stack([one, total - one])
    lengths = jnp.asarray(length_profile(count, total, reach, lean), jnp.int32)
    pairs = (count - 1) // 2
    giver, taker = lengths[1:1 + 2 * pairs:2], lengths[2:2 + 2 * pairs:2]
    margin = jnp.minimum(giver - 1, reach - taker)
    moved = jax.random.randint(jax.random.fold_in(key, 1), (pairs,), 0, 1 << 20) % (margin + 1)
    lengths = lengths.at[1:1 + 2 * pairs:2].set(giver - moved).at[2:2 + 2 * pairs:2].set(taker + moved)
    return lengths[jax.random.permutation(jax.random.fold_in(key, 2), count)]


def scatter_about(stream_key, dims, deviation, reach, split=(), kind=jnp.bfloat16):
    level = steps_of(stream_key, dims, split, -0.22, 0.18) if split else 1.0
    entries = jax.random.normal(stream_key, dims, jnp.float32) * deviation * level
    return jnp.minimum(jnp.maximum(entries, -reach), reach).astype(kind)


def setup_inputs(seed: int = 0) -> dict:
    splits = jax.random.split(jax.random.key(seed), 8)
    return {
        "tokens": scatter_about(splits[0], (N_GROUP, SEQ, D), 1.0, 6.0, ((0, 4), (1, 4))),
        "gain": jnp.clip(1.0 + 0.18 * jax.random.normal(splits[1], (D,), jnp.float32), 0.1, 1.9),
        "q_weight": scatter_about(splits[2], (D, HEADS * HEAD_DIM), D ** -0.5, 0.109375, ((0, 16), (1, 2))),
        "kv_weight": scatter_about(splits[3], (D, 2 * KV_HEADS * HEAD_DIM), D ** -0.5, 0.109375, ((0, 16), (1, 2))),
        "out_weight": scatter_about(splits[4], (HEADS * HEAD_DIM, D), (HEADS * HEAD_DIM // 16) ** -0.5, 0.5, ((0, 4), (1, 2))),
        "sinks": jnp.clip(-1.0 + 4.0 * jax.random.uniform(splits[5], (HEADS,), jnp.float32) ** steps_of(splits[5], (HEADS,), ((0, 2),), -0.2, 0.2), -1.0, 3.0),
        "segments": jax.vmap(lambda own: jnp.searchsorted(jnp.cumsum(ragged_sizes(own, DOCS, SEQ, DOC_MOST, 2)), jnp.arange(SEQ), side="right"))(jax.random.split(splits[6], N_GROUP)).reshape((N_GROUP, SEQ)).astype(jnp.int32),
    }


def rotate(vectors, positions):
    half_dim = HEAD_DIM // 2
    frequency = jnp.exp(-jnp.log(150000.0) * jnp.arange(half_dim, dtype=jnp.float32) / half_dim)
    angle = positions[:, None] * frequency[None, :]
    cosine = jnp.cos(angle)[:, None, :]
    sine = jnp.sin(angle)[:, None, :]
    first_half = vectors[..., :half_dim]
    second_half = vectors[..., half_dim:]
    return jnp.concatenate([first_half * cosine - second_half * sine, second_half * cosine + first_half * sine], axis=-1)

def reference(tokens, gain, q_weight, kv_weight, out_weight, sinks, segments):
    group_size = HEADS // KV_HEADS
    positions = jnp.arange(SEQ, dtype=jnp.float32)
    window = DOC_MOST + TOK_DEV
    sink_terms = jnp.exp(sinks).reshape(KV_HEADS, group_size)

    def one_group(inputs):
        feature, doc_ids = inputs
        widened = feature.astype(jnp.float32)
        normed = (widened * lax.rsqrt(lax.optimization_barrier(jnp.mean(widened * widened, axis=-1, keepdims=True)) + 1e-05) * gain).astype(jnp.bfloat16)
        queries = jnp.dot(normed, q_weight, preferred_element_type=jnp.float32).reshape(SEQ, HEADS, HEAD_DIM)
        queries = rotate(queries, positions).astype(jnp.bfloat16)
        paired = jnp.dot(normed, kv_weight, preferred_element_type=jnp.float32).reshape(SEQ, KV_HEADS, 2, HEAD_DIM)
        key_rows = rotate(paired[:, :, 0], positions).astype(jnp.bfloat16)
        value_rows = paired[:, :, 1].astype(jnp.bfloat16)

        def one_block(block_index):
            start = (block_index * TOK_DEV).astype(jnp.int32)
            key_start = jnp.clip(start - DOC_MOST, 0, SEQ - window).astype(jnp.int32)
            query_block = lax.dynamic_slice_in_dim(queries, start, TOK_DEV, 0).reshape(TOK_DEV, KV_HEADS, group_size, HEAD_DIM)
            key_block = lax.dynamic_slice_in_dim(key_rows, key_start, window, 0)
            value_block = lax.dynamic_slice_in_dim(value_rows, key_start, window, 0)
            query_docs = lax.dynamic_slice_in_dim(doc_ids, start, TOK_DEV, 0)
            key_docs = lax.dynamic_slice_in_dim(doc_ids, key_start, window, 0)
            query_pos = start + jnp.arange(TOK_DEV, dtype=jnp.int32)
            key_pos = key_start + jnp.arange(window, dtype=jnp.int32)
            allowed = (key_pos[None, :] <= query_pos[:, None]) & (key_docs[None, :] == query_docs[:, None])
            scores = jnp.einsum('tkgd,nkd->kgtn', query_block.astype(jnp.float32), key_block.astype(jnp.float32)) * 0.125
            weights = jnp.where(allowed[None, None], jnp.exp(scores), 0.0)
            denoms = lax.optimization_barrier(jnp.sum(weights, axis=-1)) + sink_terms[:, :, None]
            rounded = lax.optimization_barrier(weights.astype(jnp.bfloat16))
            summed = jnp.einsum('kgtn,nkd->tkgd', rounded.astype(jnp.float32), value_block.astype(jnp.float32))
            context = summed / jnp.transpose(denoms, (2, 0, 1))[..., None]
            return context.astype(jnp.bfloat16).reshape(TOK_DEV, HEADS * HEAD_DIM)
        context = lax.map(one_block, jnp.arange(SEQ // TOK_DEV, dtype=jnp.int32)).reshape(SEQ, HEADS * HEAD_DIM)
        return jnp.dot(context, out_weight, preferred_element_type=jnp.float32).astype(jnp.bfloat16)
    return lax.map(one_group, (tokens, segments))
```

```python
import math

import jax
import jax.numpy as jnp
from jax import lax
from jax.experimental import pallas as pl
from jax.experimental.pallas import tpu as pltpu
from jax.sharding import PartitionSpec as P

HEAD_DIM = 64
HALF = HEAD_DIM // 2
LANES = 128
BF16 = jnp.bfloat16
F32 = jnp.float32


VMEM = pl.BlockSpec(memory_space=pltpu.VMEM)
SMEM = pl.BlockSpec(memory_space=pltpu.SMEM)
BIG = pltpu.CompilerParams(vmem_limit_bytes=60 << 20)


def call(body, outs, args, specs, scratch=(), flops=0, moved=0, name=None):
    return pl.pallas_call(
        body,
        out_shape=outs,
        in_specs=specs,
        out_specs=jax.tree.map(lambda _: VMEM, outs),
        scratch_shapes=scratch,
        compiler_params=BIG,
        cost_estimate=pl.CostEstimate(flops=flops, bytes_accessed=moved, transcendentals=0),
        name=name,
    )(*args)


def swap(array, axis, size, mask):
    return lax.ppermute(array, axis, [(i, i ^ mask) for i in range(size)])


def contract(left, right):
    return lax.dot_general(left, right, (((0,), (0,)), ((), ())), preferred_element_type=F32)


def make_step(mesh):
    n_group, n_tensor, n_role = mesh.shape["group"], mesh.shape["tensor"], mesh.shape["role"]

    def on_device(tokens, gain, q_weight, kv_weight, out_weight, sinks, segments):
        block = tokens.shape[1]
        width = tokens.shape[2]
        rows, q_cols = q_weight.shape
        pair_cols = kv_weight.shape[1]
        pairs = pair_cols // (2 * HEAD_DIM)
        inner = 2 * pairs
        outer = n_role // inner
        pieces = n_group * n_role
        padded = -(-rows // 16) * 16
        cols = q_cols // inner
        heads = cols // HEAD_DIM
        half_cols = cols // 2
        half_heads = heads // 2
        span = inner * block
        seq = n_role * block
        out_rows, out_cols = out_weight.shape
        split = n_tensor if inner > 2 and block % (LANES * n_tensor) == 0 else 1
        part = block // split

        group = lax.axis_index("group")
        plane = lax.axis_index("tensor")
        role = lax.axis_index("role")
        mine = role % inner
        ring = role // inner
        place = jnp.stack([mine, plane, ring]).astype(jnp.int32)

        def pack_body(at, q_ref, kv_ref, *outs):
            for k in range(inner):
                target = at[0] ^ k
                outs[k][...] = jnp.zeros_like(outs[k])
                outs[k][:rows, :cols] = q_ref[:, pl.ds(pl.multiple_of(target * cols, LANES), cols)]
                pair = kv_ref[:, pl.ds(pl.multiple_of((target // 2) * LANES, LANES), LANES)]
                chosen = jnp.where(target % 2 == 0, pair[:, :HEAD_DIM], pair[:, HEAD_DIM:])
                outs[k][:rows, cols : cols + HEAD_DIM] = chosen

        packed = call(
            pack_body,
            [jax.ShapeDtypeStruct((padded, cols + LANES), BF16)] * inner,
            (place, q_weight, kv_weight),
            [SMEM, VMEM, VMEM],
            name="pack",
        )
        got = [packed[0]] + [swap(packed[k], "role", n_role, k) for k in range(1, inner)]

        def stack_body(at, *refs):
            sources, (kv_out, left_out, right_out) = refs[:inner], refs[inner:]
            for k in range(inner):
                spot = at[0] ^ k
                left_out[spot] = sources[k][:, :half_cols]
                right_out[spot] = sources[k][:, half_cols:cols]
            for m in range(inner // 2):
                spot = (at[0] // 2) ^ m
                one = sources[2 * m][:, cols : cols + HEAD_DIM]
                two = sources[2 * m + 1][:, cols : cols + HEAD_DIM]
                even = at[0] % 2 == 0
                kv_out[spot] = jnp.concatenate(
                    [jnp.where(even, one, two), jnp.where(even, two, one)], axis=1
                )

        held = call(
            stack_body,
            [
                jax.ShapeDtypeStruct((inner // 2, padded, LANES), BF16),
                jax.ShapeDtypeStruct((inner, padded, half_cols), BF16),
                jax.ShapeDtypeStruct((inner, padded, half_cols), BF16),
            ],
            (place, *got),
            [SMEM] + [VMEM] * inner,
            name="stack",
        )

        def over_outer(array):
            steps = [array]
            for o in range(1, outer):
                ahead = [(i, (i + o * inner) % n_role) for i in range(n_role)]
                steps.append(lax.ppermute(array, "role", ahead))
            return steps

        forward = [(i, (i + 1) % n_group) for i in range(n_group)]
        current = [over_outer(array) for array in held]
        rings = [[array] for array in current]
        for _ in range(1, n_group):
            current = [[lax.ppermute(x, "group", forward) for x in array] for array in current]
            for a, array in enumerate(current):
                rings[a].append(array)
        where = jnp.stack(
            [
                ((group - s) % n_group) * outer + (ring - o) % outer
                for s in range(n_group)
                for o in range(outer)
            ]
        ).astype(jnp.int32)
        kv_parts, left_parts, right_parts = [[x for s in r for x in s] for r in rings]
        count = n_group * outer

        wide_gain = jnp.broadcast_to(gain[:, None], (width, LANES))

        def norm_body(at, x_ref, g_ref, out_ref, *rest):
            part_refs, wide_ref = rest[:-1], rest[-1]
            wide = x_ref[...].astype(F32)
            wide_ref[...] = wide
            scale = lax.rsqrt(jnp.sum(wide * wide, axis=0, keepdims=True) / width + 1e-05)
            for p in range(pieces):
                pick = pl.ds(p * rows, rows)
                for c in range(block // LANES):
                    lanes = slice(c * LANES, (c + 1) * LANES)
                    value = wide_ref[pick, lanes] * scale[:, lanes] * g_ref[pick, :]
                    out_ref[p, :rows, lanes] = value.astype(BF16)
                    if padded > rows:
                        out_ref[p, rows:, lanes] = jnp.zeros((padded - rows, LANES), BF16)
                for ref in part_refs:
                    ref[p] = out_ref[p, :, pl.ds(pl.multiple_of(at[1] * part, LANES), part)]

        shapes = [jax.ShapeDtypeStruct((pieces, padded, block), BF16)]
        if split > 1:
            shapes.append(jax.ShapeDtypeStruct((pieces, padded, part), BF16))
        own, *own_part = call(
            norm_body,
            shapes,
            (place, tokens[0].T, wide_gain),
            [SMEM, VMEM, VMEM],
            scratch=[pltpu.VMEM((width, block), F32)],
            name="norm",
        )
        blocks = [(0, None, own)]
        bit = inner // 2
        while bit:
            if bit > 1 and split > 1 and len(blocks) == 1:
                piece = swap(own_part[0], "role", n_role, bit)
                blocks.append((bit, 0, piece))
                for t in range(1, split):
                    after = [(i, (i + 1) % split) for i in range(split)]
                    piece = lax.ppermute(piece, "tensor", after)
                    blocks.append((bit, t, piece))
            else:
                blocks += [(m ^ bit, t, swap(x, "role", n_role, bit)) for m, t, x in blocks]
            bit //= 2

        def join_body(at, *refs):
            out_ref = refs[-1]
            for ref, (m, t, _) in zip(refs, blocks):
                start = (at[0] ^ m) * block
                if t is not None:
                    start = start + ((at[1] + split - t) % split) * part
                size = ref.shape[2]
                out_ref[:, :, pl.ds(pl.multiple_of(start, LANES), size)] = ref[...]

        normed = call(
            join_body,
            jax.ShapeDtypeStruct((pieces, padded, span), BF16),
            (place, *[x for _, _, x in blocks]),
            [SMEM] + [VMEM] * len(blocks),
            name="join",
        ).reshape(n_group * outer, inner * padded, span)
        depth = inner * padded

        positions = (ring * span + jnp.arange(span, dtype=jnp.int32)).astype(F32)
        frequency = jnp.exp(-jnp.log(150000.0) * jnp.arange(HALF, dtype=F32) / HALF)
        angle = frequency[:, None] * positions[None, :]
        turn = jnp.stack([jnp.cos(angle), jnp.sin(angle)])

        tile = math.gcd(span, 256)

        def rotated(vector, turn_ref, at):
            a, b = vector[:HALF], vector[HALF:]
            cosine, sine = turn_ref[0, :, at], turn_ref[1, :, at]
            return jnp.concatenate([a * cosine - b * sine, b * cosine + a * sine], axis=0)

        def kv_body(at, where_ref, turn_ref, x_ref, *refs):
            weights, out_ref, full = refs[:count], refs[count], refs[count + 1]
            for i in range(count):
                for m in range(inner // 2):
                    full[i, 2 * m] = weights[i][m, :, :HEAD_DIM]
                    full[i, 2 * m + 1] = weights[i][m, :, HEAD_DIM:]
            for t in range(span // tile):
                lanes = slice(t * tile, (t + 1) * tile)
                total = jnp.zeros((HEAD_DIM, tile), F32)
                for i in range(count):
                    total = total + contract(
                        full[i].reshape(depth, HEAD_DIM), x_ref[where_ref[i], :, lanes]
                    )
                turned = rotated(total, turn_ref, lanes)
                out_ref[:, lanes] = jnp.where(at[0] % 2 == 0, turned, total).astype(BF16)

        kv_mine = call(
            kv_body,
            jax.ShapeDtypeStruct((HEAD_DIM, span), BF16),
            (place, where, turn, normed, *kv_parts),
            [SMEM, SMEM, VMEM, VMEM] + [VMEM] * count,
            scratch=[pltpu.VMEM((count, inner, padded, HEAD_DIM), BF16)],
            flops=2 * count * depth * HEAD_DIM * span,
            name="keys_values",
        )
        if outer == 1:
            kv_other = swap(kv_mine, "role", n_role, 1)
            even = mine % 2 == 0
            keys = jnp.where(even, kv_mine, kv_other)
            values = jnp.where(even, kv_other, kv_mine)
        else:
            both = lax.all_gather(kv_mine, "role", axis=0).reshape(outer, inner, HEAD_DIM, span)

            def along(index):
                taken = lax.dynamic_index_in_dim(both, index, 1, keepdims=False)
                return jnp.swapaxes(taken, 0, 1).reshape(HEAD_DIM, seq)

            keys, values = along((mine // 2) * 2), along((mine // 2) * 2 + 1)

        def q_sum(where_ref, x_ref, lefts, rights, offset, lanes):
            total = None
            for i in range(len(lefts)):
                weight = jnp.concatenate([lefts[i][...], rights[i][...]], axis=2)
                added = contract(
                    weight.reshape(depth, cols), x_ref[where_ref[offset + i], :, lanes]
                )
                total = added if total is None else total + added
            return total

        early = count - outer

        def q_early_body(where_ref, x_ref, *refs):
            lefts, rights, out_ref = refs[:early], refs[early : 2 * early], refs[2 * early]
            for t in range(span // tile):
                lanes = slice(t * tile, (t + 1) * tile)
                out_ref[:, lanes] = q_sum(where_ref, x_ref, lefts, rights, 0, lanes)

        q_begun = call(
            q_early_body,
            jax.ShapeDtypeStruct((cols, span), F32),
            (where, normed, *left_parts[:early], *right_parts[:early]),
            [SMEM, VMEM] + [VMEM] * (2 * early),
            flops=2 * early * depth * cols * span,
            name="queries_early",
        )

        def q_late_body(where_ref, turn_ref, x_ref, begun_ref, *refs):
            lefts, rights, out_ref = refs[:outer], refs[outer : 2 * outer], refs[2 * outer]
            for t in range(span // tile):
                lanes = slice(t * tile, (t + 1) * tile)
                total = begun_ref[:, lanes] + q_sum(where_ref, x_ref, lefts, rights, early, lanes)
                for h in range(heads):
                    here = slice(h * HEAD_DIM, (h + 1) * HEAD_DIM)
                    out_ref[here, lanes] = (0.125 * rotated(total[here], turn_ref, lanes)).astype(
                        BF16
                    )

        queries = call(
            q_late_body,
            jax.ShapeDtypeStruct((cols, span), BF16),
            (where, turn, normed, q_begun, *left_parts[early:], *right_parts[early:]),
            [SMEM, VMEM, VMEM, VMEM] + [VMEM] * (2 * outer),
            flops=2 * outer * depth * cols * span,
            name="queries_late",
        )

        gathered = [(0, segments)]
        weights_out = [(0, out_weight.T)]
        bit = n_role // 2
        while bit:
            gathered += [(m ^ bit, swap(x, "role", n_role, bit)) for m, x in gathered]
            weights_out += [(m ^ bit, swap(x, "role", n_role, bit)) for m, x in weights_out]
            bit //= 2
        docs = jnp.zeros((n_role, block), jnp.int32)
        for m, x in gathered:
            docs = lax.dynamic_update_slice(docs, x, (role ^ m, 0))
        docs = docs.reshape(seq)
        own_docs = lax.dynamic_slice(docs, (ring * span,), (span,))
        first = jnp.sum((docs[:, None] < own_docs[None, :]).astype(jnp.int32), axis=0)
        lowest = first[::block] // block
        first = first[None, :]
        sink_terms = jnp.exp(sinks)

        def attend_body(at, lowest_ref, sink_ref, first_ref, q_ref, k_ref, v_ref, out_ref, half):
            base = half * half_heads
            for qb in range(inner):
                lanes = slice(qb * block, (qb + 1) * block)
                start = first_ref[:, lanes]
                last = at[2] * inner + qb
                pos = last * block + lax.broadcasted_iota(jnp.int32, (1, block), 1)
                qs = [
                    q_ref[(base + h) * HEAD_DIM : (base + h + 1) * HEAD_DIM, lanes]
                    for h in range(half_heads)
                ]

                def advance(kb, carry):
                    at_key = pl.multiple_of(kb * block, LANES)
                    k = k_ref[:, pl.ds(at_key, block)]
                    v = v_ref[:, pl.ds(at_key, block)]
                    index = kb * block + lax.broadcasted_iota(jnp.int32, (block, block), 0)
                    allowed = (index >= start) & (index <= pos)
                    after = []
                    for h in range(half_heads):
                        total, summed = carry[h]
                        weight = jnp.where(allowed, jnp.exp(contract(k, qs[h])), 0.0)
                        total = total + jnp.sum(weight, axis=0, keepdims=True)
                        summed = summed + jnp.dot(
                            v, weight.astype(BF16), preferred_element_type=F32
                        )
                        after.append((total, summed))
                    return tuple(after)

                zero = (jnp.zeros((1, block), F32), jnp.zeros((HEAD_DIM, block), F32))
                done = lax.fori_loop(lowest_ref[qb], last + 1, advance, (zero,) * half_heads)
                for h in range(half_heads):
                    total, summed = done[h]
                    total = total + sink_ref[at[0] * heads + base + h]
                    here = slice(h * HEAD_DIM, (h + 1) * HEAD_DIM)
                    out_ref[qb, here, :] = (summed / total).astype(BF16)

        def attend(half):
            def body(*refs):
                attend_body(*refs, half)

            return call(
                body,
                jax.ShapeDtypeStruct((inner, half_cols, block), BF16),
                (place, lowest, sink_terms, first, queries, keys, values),
                [SMEM, SMEM, SMEM] + [VMEM] * 4,
                flops=half_heads * 4 * HEAD_DIM * span * seq // 2,
                name="attend",
            )

        def exchange(context):
            if outer == 1:
                sent = jnp.concatenate([context] * n_tensor, axis=0)
                return lax.all_to_all(sent, ("tensor", "role"), 0, 0, tiled=True)
            pieces_in = []
            for k in range(inner):
                piece = lax.dynamic_index_in_dim(context, mine ^ k, 0, keepdims=False)
                pieces_in.append(swap(piece, "role", n_role, k) if k else piece)
            stacked = jnp.stack(pieces_in)
            ordered = jnp.stack(
                [lax.dynamic_index_in_dim(stacked, mine ^ i, 0, keepdims=False) for i in range(inner)]
            )
            every = lax.all_gather(ordered, "tensor", axis=0)
            return every.reshape(n_tensor * inner, half_cols, block)

        context = [exchange(attend(half)) for half in range(2)]

        table = jnp.stack([role ^ m for m, _ in weights_out]).astype(jnp.int32)

        def out_body(table_ref, one_ref, two_ref, *refs):
            weights, out_ref, nat = refs[:n_role], refs[n_role], refs[n_role + 1]
            for i in range(n_tensor * inner):
                nat[i * cols : i * cols + half_cols] = one_ref[i]
                nat[i * cols + half_cols : (i + 1) * cols] = two_ref[i]
            total = None
            for k in range(n_role):
                rows_at = pl.ds(pl.multiple_of(table_ref[k] * out_rows, LANES), out_rows)
                added = jnp.dot(weights[k][...], nat[rows_at, :], preferred_element_type=F32)
                total = added if total is None else total + added
            out_ref[...] = total.astype(BF16)

        mixed = call(
            out_body,
            jax.ShapeDtypeStruct((out_cols, block), BF16),
            (table, *context, *[x for _, x in weights_out]),
            [SMEM] + [VMEM] * (2 + n_role),
            scratch=[pltpu.VMEM((n_role * out_rows, block), BF16)],
            flops=2 * n_role * out_rows * out_cols * block,
            name="mix",
        )
        return mixed.T[None]

    return on_device


def solution(mesh):
    placed = (
        P("group", "role", None),
        P(),
        P(("group", "role"), "tensor"),
        P(("group", "role"), "tensor"),
        P("role", "tensor"),
        P("tensor"),
        P("group", "role"),
    )
    return jax.shard_map(
        make_step(mesh),
        mesh=mesh,
        in_specs=placed,
        out_specs=P("group", "role", "tensor"),
        check_vma=False,
    )
```

```python
import math

import jax
import jax.numpy as jnp
from jax import lax
from jax.experimental import pallas as pl
from jax.experimental.pallas import tpu as pltpu
from jax.sharding import PartitionSpec as P

HEAD_DIM = 64
HALF = HEAD_DIM // 2
LANES = 128
BF16 = jnp.bfloat16
F32 = jnp.float32


VMEM = pl.BlockSpec(memory_space=pltpu.VMEM)
SMEM = pl.BlockSpec(memory_space=pltpu.SMEM)
ANY = pl.BlockSpec(memory_space=pl.ANY)


def call(body, outs, args, specs, scratch=(), flops=0, moved=0, name=None, limit=16):
    return pl.pallas_call(
        body,
        out_shape=outs,
        in_specs=specs,
        out_specs=jax.tree.map(lambda _: VMEM, outs),
        scratch_shapes=scratch,
        compiler_params=pltpu.CompilerParams(vmem_limit_bytes=limit << 20),
        cost_estimate=pl.CostEstimate(flops=flops, bytes_accessed=moved, transcendentals=0),
        name=name,
    )(*args)


def swap(array, axis, size, mask):
    return lax.ppermute(array, axis, [(i, i ^ mask) for i in range(size)])


def contract(left, right):
    return lax.dot_general(left, right, (((0,), (0,)), ((), ())), preferred_element_type=F32)


def make_step(mesh):
    n_group, n_tensor, n_role = mesh.shape["group"], mesh.shape["tensor"], mesh.shape["role"]

    def on_device(tokens, gain, q_weight, kv_weight, out_weight, sinks, segments):
        block = tokens.shape[1]
        width = tokens.shape[2]
        rows, q_cols = q_weight.shape
        pair_cols = kv_weight.shape[1]
        pairs = pair_cols // (2 * HEAD_DIM)
        inner = 2 * pairs
        outer = n_role // inner
        cols = q_cols // inner
        heads = cols // HEAD_DIM
        half_cols = cols // 2
        half_heads = heads // 2
        span = inner * block
        seq = n_role * block
        out_rows, out_cols = out_weight.shape
        split = n_tensor if inner > 2 and width % (16 * n_tensor) == 0 else 1
        part = width // split

        group = lax.axis_index("group")
        plane = lax.axis_index("tensor")
        role = lax.axis_index("role")
        mine = role % inner
        ring = role // inner
        place = jnp.stack([mine, plane, ring]).astype(jnp.int32)

        wide = cols + LANES

        def pack_body(at, q_ref, kv_ref, *outs):
            for k in range(inner):
                target = at[0] ^ k
                outs[k][:, :cols] = q_ref[:, pl.ds(pl.multiple_of(target * cols, LANES), cols)]
                pair = kv_ref[:, pl.ds(pl.multiple_of((target // 2) * LANES, LANES), LANES)]
                chosen = jnp.where(target % 2 == 0, pair[:, :HEAD_DIM], pair[:, HEAD_DIM:])
                outs[k][:, cols : cols + HEAD_DIM] = chosen
                outs[k][:, cols + HEAD_DIM :] = jnp.zeros((rows, HEAD_DIM), BF16)

        packed = call(
            pack_body,
            [jax.ShapeDtypeStruct((rows, wide), BF16)] * inner,
            (place, q_weight, kv_weight),
            [SMEM, VMEM, VMEM],
            name="pack",
            limit=6,
        )
        got = [packed[0]] + [swap(packed[k], "role", n_role, k) for k in range(1, inner)]
        sources = [(0, k, x) for k, x in enumerate(got)]
        for o in range(1, outer):
            ahead = [(i, (i + o * inner) % n_role) for i in range(n_role)]
            sources += [(o, k, lax.ppermute(x, "role", ahead)) for k, x in enumerate(got)]

        deep = n_role * rows
        kv_deep = -(-deep // 32) * 16
        own_gain = lax.dynamic_slice(gain, (group * deep,), (deep,))
        own_gain = jnp.broadcast_to(own_gain[:, None], (deep, LANES))

        def stack_body(at, gain_ref, *refs):
            kv_out, left_out, right_out, one, two = refs[n_role:]
            for ref, (o, k, _) in zip(refs[:n_role], sources):
                spot = lax.rem(at[2] + outer - o, outer) * inner + (at[0] ^ k)
                one[spot, :rows, :] = ref[...].astype(F32)
            for p in range(n_role):
                two[p * rows : (p + 1) * rows, :] = one[p, :rows, :]
            for out_ref, c in ((left_out, 0), (right_out, half_cols)):
                for lane in range(0, half_cols, LANES):
                    here = slice(lane, lane + LANES)
                    there = slice(c + lane, c + lane + LANES)
                    out_ref[:, here] = (two[:, there] * gain_ref[...]).astype(BF16)
            kv = (two[:, cols:] * gain_ref[...])[:, :HEAD_DIM].astype(BF16)
            kv_out[...] = jnp.zeros_like(kv_out)
            kv_out[:, :HEAD_DIM] = kv[:kv_deep]
            kv_out[: deep - kv_deep, HEAD_DIM:] = kv[kv_deep:]

        held = call(
            stack_body,
            [
                jax.ShapeDtypeStruct((kv_deep, LANES), BF16),
                jax.ShapeDtypeStruct((deep, half_cols), BF16),
                jax.ShapeDtypeStruct((deep, half_cols), BF16),
            ],
            (place, own_gain, *[x for _, _, x in sources]),
            [SMEM, VMEM] + [VMEM] * n_role,
            scratch=[
                pltpu.VMEM((n_role, -(-rows // 8) * 8, wide), F32),
                pltpu.VMEM((deep, wide), F32),
            ],
            name="stack",
            limit=12,
        )

        forward = [(i, (i + 1) % n_group) for i in range(n_group)]
        rings = [[array] for array in held]
        for _ in range(1, n_group):
            for array in rings:
                array.append(lax.ppermute(array[-1], "group", forward))
        kv_parts, left_parts, right_parts = rings
        where = jnp.stack([(group - s) % n_group for s in range(n_group)]).astype(jnp.int32)

        own = tokens[0].T
        blocks = [(0, None, own)]
        bit = inner // 2
        while bit:
            if bit > 1 and split > 1 and len(blocks) == 1:
                piece = lax.dynamic_slice(own, (plane * part, 0), (part, block))
                piece, _ = lax.optimization_barrier((piece, packed[1]))
                piece = swap(piece, "role", n_role, bit)
                blocks.append((bit, 0, piece))
                for t in range(1, split):
                    after = [(i, (i + 1) % split) for i in range(split)]
                    piece = lax.ppermute(piece, "tensor", after)
                    blocks.append((bit, t, piece))
                last_token = blocks[1][2]
            else:
                blocks += [(m ^ bit, t, swap(x, "role", n_role, bit)) for m, t, x in blocks]
            bit //= 2

        positions = (ring * span + jnp.arange(span, dtype=jnp.int32)).astype(F32)
        frequency = jnp.exp(-jnp.log(150000.0) * jnp.arange(HALF, dtype=F32) / HALF)
        angle = frequency[:, None] * positions[None, :]
        turn = jnp.stack([jnp.cos(angle), jnp.sin(angle)])

        tile = math.gcd(span, 256)

        def rotated(vector, turn_ref, at):
            a, b = vector[:HALF], vector[HALF:]
            cosine, sine = turn_ref[0, :, at], turn_ref[1, :, at]
            return jnp.concatenate([a * cosine - b * sine, b * cosine + a * sine], axis=0)

        early = n_group - 1
        n_blocks = len(blocks)

        def early_body(at, where_ref, turn_ref, *refs):
            parts, refs = refs[:n_blocks], refs[n_blocks:]
            kv_refs, refs = refs[:n_group], refs[n_group:]
            lefts, rights, refs = refs[:early], refs[early : 2 * early], refs[2 * early :]
            kv_out, begun_out, scale_out, late_out, x, full, sems = refs
            copies = []
            for i, (ref, (m, t, _)) in enumerate(zip(parts, blocks)):
                start = pl.multiple_of((at[0] ^ m) * block, LANES)
                first_row = 0
                if t is not None:
                    first_row = pl.multiple_of(lax.rem(at[1] + split - t, split) * part, 16)
                target = x.at[pl.ds(first_row, ref.shape[0]), pl.ds(start, block)]
                copies.append(pltpu.make_async_copy(ref, target, sems.at[i]))
                copies[-1].start()
            full[...] = jnp.zeros_like(full)
            for s in range(n_group):
                full[s, :kv_deep, :HEAD_DIM] = kv_refs[s][:, :HEAD_DIM]
                full[s, kv_deep:, :HEAD_DIM] = kv_refs[s][: deep - kv_deep, HEAD_DIM:]
            for copy in copies:
                copy.wait()
            spots = [pl.ds(pl.multiple_of(where_ref[s] * deep, 16), deep) for s in range(n_group)]
            late_out[...] = x[spots[early], :]
            for t in range(span // tile):
                lanes = slice(t * tile, (t + 1) * tile)
                squares = jnp.zeros((1, tile), F32)
                for s in range(n_group):
                    piece = x[s * deep : (s + 1) * deep, lanes].astype(F32)
                    squares = squares + jnp.sum(piece * piece, axis=0, keepdims=True)
                scale = lax.rsqrt(squares / width + 1e-05)
                scale_out[:, lanes] = scale
                total = contract(full[early], x[spots[early], lanes])[:HEAD_DIM]
                begun = None
                for s in range(early):
                    weight = jnp.concatenate([lefts[s][...], rights[s][...], full[s]], axis=1)
                    added = contract(weight, x[spots[s], lanes])
                    total = total + added[cols : cols + HEAD_DIM]
                    begun = added[:cols] if begun is None else begun + added[:cols]
                begun_out[:, lanes] = begun
                total = total * scale
                turned = rotated(total, turn_ref, lanes)
                kv_out[:, lanes] = jnp.where(at[0] % 2 == 0, turned, total).astype(BF16)

        kv_mine, begun, scales, x_late = call(
            early_body,
            [
                jax.ShapeDtypeStruct((HEAD_DIM, span), BF16),
                jax.ShapeDtypeStruct((cols, span), F32),
                jax.ShapeDtypeStruct((1, span), F32),
                jax.ShapeDtypeStruct((deep, span), BF16),
            ],
            (
                place,
                where,
                turn,
                *[x for _, _, x in blocks],
                *kv_parts,
                *left_parts[:early],
                *right_parts[:early],
            ),
            [SMEM, SMEM, VMEM] + [ANY] * n_blocks + [VMEM] * (n_group + 2 * early),
            scratch=[
                pltpu.VMEM((width, span), BF16),
                pltpu.VMEM((n_group, deep, LANES), BF16),
                pltpu.SemaphoreType.DMA((n_blocks,)),
            ],
            flops=2 * width * (cols + HEAD_DIM) * span,
            name="early",
            limit=28,
        )
        if outer == 1:
            kv_pair = (kv_mine, swap(kv_mine, "role", n_role, 1))
            flip = mine % 2
        else:
            both = lax.all_gather(kv_mine, "role", axis=0).reshape(outer, inner, HEAD_DIM, span)

            def along(index):
                taken = lax.dynamic_index_in_dim(both, index, 1, keepdims=False)
                return jnp.swapaxes(taken, 0, 1).reshape(HEAD_DIM, seq)

            kv_pair = (along((mine // 2) * 2), along((mine // 2) * 2 + 1))
            flip = jnp.int32(0)

        def late_body(turn_ref, scale_ref, x_ref, begun_ref, left_ref, right_ref, out_ref):
            weight = jnp.concatenate([left_ref[...], right_ref[...]], axis=1)
            for t in range(span // tile):
                lanes = slice(t * tile, (t + 1) * tile)
                total = begun_ref[:, lanes] + contract(weight, x_ref[:, lanes])
                total = total * (scale_ref[:, lanes] * 0.125)
                for h in range(heads):
                    here = slice(h * HEAD_DIM, (h + 1) * HEAD_DIM)
                    out_ref[here, lanes] = rotated(total[here], turn_ref, lanes).astype(BF16)

        queries = call(
            late_body,
            jax.ShapeDtypeStruct((cols, span), BF16),
            (turn, scales, x_late, begun, left_parts[early], right_parts[early]),
            [VMEM] * 6,
            flops=2 * deep * cols * span,
            name="late",
            limit=12,
        )

        shared = out_weight.T
        if split > 1:
            shared, _ = lax.optimization_barrier((shared, last_token))
        gathered = [(0, segments)]
        weights_out = [(0, shared)]
        bit = n_role // 2
        while bit:
            gathered += [(m ^ bit, swap(x, "role", n_role, bit)) for m, x in gathered]
            weights_out += [(m ^ bit, swap(x, "role", n_role, bit)) for m, x in weights_out]
            bit //= 2
        docs = jnp.zeros((n_role, block), jnp.int32)
        for m, x in gathered:
            docs = lax.dynamic_update_slice(docs, x, (role ^ m, 0))
        docs = docs.reshape(seq)
        own_docs = lax.dynamic_slice(docs, (ring * span,), (span,))
        first = jnp.sum((docs[:, None] < own_docs[None, :]).astype(jnp.int32), axis=0)
        lowest = first[::block] // block
        first = first[None, :]
        sink_terms = jnp.exp(sinks)
        turns = jnp.stack([mine, flip, ring]).astype(jnp.int32)

        copies_out = n_tensor if outer == 1 else 1

        def attend_body(
            at, lowest_ref, sink_ref, first_ref, q_ref, a_ref, b_ref, out_ref, k_ref, v_ref, half
        ):
            base = half * half_heads
            k_ref[...] = jnp.where(at[1] == 0, a_ref[...], b_ref[...])
            v_ref[...] = jnp.where(at[1] == 0, b_ref[...], a_ref[...])
            for qb in range(inner):
                lanes = slice(qb * block, (qb + 1) * block)
                start = first_ref[:, lanes]
                last = at[2] * inner + qb
                pos = last * block + lax.broadcasted_iota(jnp.int32, (1, block), 1)
                qs = [
                    q_ref[(base + h) * HEAD_DIM : (base + h + 1) * HEAD_DIM, lanes]
                    for h in range(half_heads)
                ]

                def advance(kb, carry):
                    at_key = pl.multiple_of(kb * block, LANES)
                    k = k_ref[:, pl.ds(at_key, block)]
                    v = v_ref[:, pl.ds(at_key, block)]
                    index = kb * block + lax.broadcasted_iota(jnp.int32, (block, block), 0)
                    allowed = (index >= start) & (index <= pos)
                    after = []
                    for h in range(half_heads):
                        total, summed = carry[h]
                        weight = jnp.where(allowed, jnp.exp(contract(k, qs[h])), 0.0)
                        total = total + jnp.sum(weight, axis=0, keepdims=True)
                        summed = summed + jnp.dot(
                            v, weight.astype(BF16), preferred_element_type=F32
                        )
                        after.append((total, summed))
                    return tuple(after)

                zero = (jnp.zeros((1, block), F32), jnp.zeros((HEAD_DIM, block), F32))
                done = lax.fori_loop(lowest_ref[qb], last + 1, advance, (zero,) * half_heads)
                for h in range(half_heads):
                    total, summed = done[h]
                    total = total + sink_ref[at[0] * heads + base + h]
                    here = slice(h * HEAD_DIM, (h + 1) * HEAD_DIM)
                    value = (summed / total).astype(BF16)
                    for copy in range(copies_out):
                        out_ref[copy * inner + qb, here, :] = value

        def attend(half):
            def body(*refs):
                attend_body(*refs, half)

            return call(
                body,
                jax.ShapeDtypeStruct((copies_out * inner, half_cols, block), BF16),
                (turns, lowest, sink_terms, first, queries, *kv_pair),
                [SMEM, SMEM, SMEM] + [VMEM] * 4,
                scratch=[pltpu.VMEM((HEAD_DIM, seq), BF16)] * 2,
                flops=half_heads * 4 * HEAD_DIM * span * seq // 2,
                name="attend",
            )

        def exchange(context):
            if outer == 1:
                return lax.all_to_all(context, ("tensor", "role"), 0, 0, tiled=True)
            pieces_in = []
            for k in range(inner):
                piece = lax.dynamic_index_in_dim(context, mine ^ k, 0, keepdims=False)
                pieces_in.append(swap(piece, "role", n_role, k) if k else piece)
            stacked = jnp.stack(pieces_in)
            ordered = jnp.stack(
                [lax.dynamic_index_in_dim(stacked, mine ^ i, 0, keepdims=False) for i in range(inner)]
            )
            every = lax.all_gather(ordered, "tensor", axis=0)
            return every.reshape(n_tensor * inner, half_cols, block)

        context = [exchange(attend(half)) for half in range(2)]

        table = jnp.stack([role ^ m for m, _ in weights_out]).astype(jnp.int32)

        def out_body(table_ref, one_ref, two_ref, *refs):
            weights, out_ref, nat = refs[:n_role], refs[n_role], refs[n_role + 1]
            for i in range(n_tensor * inner):
                nat[i * cols : i * cols + half_cols] = one_ref[i]
                nat[i * cols + half_cols : (i + 1) * cols] = two_ref[i]
            total = None
            for k in range(n_role):
                rows_at = pl.ds(pl.multiple_of(table_ref[k] * out_rows, LANES), out_rows)
                added = jnp.dot(weights[k][...], nat[rows_at, :], preferred_element_type=F32)
                total = added if total is None else total + added
            out_ref[...] = total.astype(BF16)

        mixed = call(
            out_body,
            jax.ShapeDtypeStruct((out_cols, block), BF16),
            (table, *context, *[x for _, x in weights_out]),
            [SMEM] + [VMEM] * (2 + n_role),
            scratch=[pltpu.VMEM((n_role * out_rows, block), BF16)],
            flops=2 * n_role * out_rows * out_cols * block,
            name="mix",
            limit=20,
        )
        return mixed.T[None]

    return on_device


def solution(mesh):
    placed = (
        P("group", "role", None),
        P(),
        P(("group", "role"), "tensor"),
        P(("group", "role"), "tensor"),
        P("role", "tensor"),
        P("tensor"),
        P("group", "role"),
    )
    return jax.shard_map(
        make_step(mesh),
        mesh=mesh,
        in_specs=placed,
        out_specs=P("group", "role", "tensor"),
        check_vma=False,
    )
```

```python
import math

import jax
import jax.numpy as jnp
from jax import lax
from jax.experimental import pallas as pl
from jax.experimental.pallas import tpu as pltpu
from jax.sharding import PartitionSpec as P


HEAD_DIM = 64
HALF = HEAD_DIM // 2
LANES = 128
BF16 = jnp.bfloat16
F32 = jnp.float32


VMEM = pl.BlockSpec(memory_space=pltpu.VMEM)
SMEM = pl.BlockSpec(memory_space=pltpu.SMEM)
ANY = pl.BlockSpec(memory_space=pl.ANY)


def call(body, outs, args, specs, scratch=(), flops=0, moved=0, limit=16):
    return pl.pallas_call(
        body,
        out_shape=outs,
        in_specs=specs,
        out_specs=jax.tree.map(lambda _: VMEM, outs),
        scratch_shapes=scratch,
        compiler_params=pltpu.CompilerParams(vmem_limit_bytes=limit << 20),
        cost_estimate=pl.CostEstimate(flops=flops, bytes_accessed=moved, transcendentals=0),
    )(*args)


def swap(array, axis, size, mask):
    return lax.ppermute(array, axis, [(i, i ^ mask) for i in range(size)])


def fetch(pairs, sems):
    copies = [pltpu.make_async_copy(a, b, sems.at[i]) for i, (a, b) in enumerate(pairs)]
    for copy in copies:
        copy.start()
    return copies


def contract(left, right):
    return lax.dot_general(left, right, (((0,), (0,)), ((), ())), preferred_element_type=F32)


def make_step(mesh):
    n_group, n_tensor, n_role = mesh.shape["group"], mesh.shape["tensor"], mesh.shape["role"]

    def on_device(tokens, gain, q_weight, kv_weight, out_weight, sinks, segments):
        block = tokens.shape[1]
        width = tokens.shape[2]
        rows, q_cols = q_weight.shape
        pair_cols = kv_weight.shape[1]
        pairs = pair_cols // (2 * HEAD_DIM)
        inner = 2 * pairs
        outer = n_role // inner
        cols = q_cols // inner
        heads = cols // HEAD_DIM
        half_cols = cols // 2
        half_heads = heads // 2
        span = inner * block
        seq = n_role * block
        out_rows, out_cols = out_weight.shape
        split = n_tensor if inner > 2 and width % (16 * n_tensor) == 0 else 1
        part = width // split

        group = lax.axis_index("group")
        plane = lax.axis_index("tensor")
        role = lax.axis_index("role")
        mine = role % inner
        ring = role // inner
        place = jnp.stack([mine, plane, ring]).astype(jnp.int32)

        wide = cols + LANES

        def pack_body(at, q_hbm, kv_hbm, *outs):
            outs, (q_ref, kv_ref, sems) = outs[:inner], outs[inner:]
            for copy in fetch([(q_hbm, q_ref), (kv_hbm, kv_ref)], sems):
                copy.wait()
            for k in range(inner):
                target = at[0] ^ k
                outs[k][:, :cols] = q_ref[:, pl.ds(pl.multiple_of(target * cols, LANES), cols)]
                pair = kv_ref[:, pl.ds(pl.multiple_of((target // 2) * LANES, LANES), LANES)]
                chosen = jnp.where(target % 2 == 0, pair[:, :HEAD_DIM], pair[:, HEAD_DIM:])
                outs[k][:, cols : cols + HEAD_DIM] = chosen
                outs[k][:, cols + HEAD_DIM :] = jnp.zeros((rows, HEAD_DIM), BF16)

        packed = call(
            pack_body,
            [jax.ShapeDtypeStruct((rows, wide), BF16)] * inner,
            (place, q_weight, kv_weight),
            [SMEM, ANY, ANY],
            scratch=[
                pltpu.VMEM(q_weight.shape, BF16),
                pltpu.VMEM(kv_weight.shape, BF16),
                pltpu.SemaphoreType.DMA((2,)),
            ],
            limit=6,
        )
        got = [packed[0]] + [swap(packed[k], "role", n_role, k) for k in range(1, inner)]
        sources = [(0, k, x) for k, x in enumerate(got)]
        for o in range(1, outer):
            ahead = [(i, (i + o * inner) % n_role) for i in range(n_role)]
            sources += [(o, k, lax.ppermute(x, "role", ahead)) for k, x in enumerate(got)]

        deep = n_role * rows
        kv_deep = -(-deep // 32) * 16
        own_gain = lax.dynamic_slice(gain, (group * deep,), (deep,))
        own_gain = jnp.broadcast_to(own_gain[:, None], (deep, LANES))

        def stack_body(at, gain_ref, *refs):
            kv_out, left_out, right_out, one, two, sems = refs[n_role:]
            pairs = []
            for ref, (o, k, _) in zip(refs[:n_role], sources):
                spot = lax.rem(at[2] + outer - o, outer) * inner + (at[0] ^ k)
                pairs.append((ref, one.at[spot]))
            for copy in fetch(pairs, sems):
                copy.wait()
            for p in range(n_role):
                two[p * rows : (p + 1) * rows, :] = one[p].astype(F32)
            for out_ref, c in ((left_out, 0), (right_out, half_cols)):
                for lane in range(0, half_cols, LANES):
                    here = slice(lane, lane + LANES)
                    there = slice(c + lane, c + lane + LANES)
                    out_ref[:, here] = (two[:, there] * gain_ref[...]).astype(BF16)
            kv = (two[:, cols:] * gain_ref[...])[:, :HEAD_DIM].astype(BF16)
            kv_out[...] = jnp.zeros_like(kv_out)
            kv_out[:, :HEAD_DIM] = kv[:kv_deep]
            kv_out[: deep - kv_deep, HEAD_DIM:] = kv[kv_deep:]

        held = call(
            stack_body,
            [
                jax.ShapeDtypeStruct((kv_deep, LANES), BF16),
                jax.ShapeDtypeStruct((deep, half_cols), BF16),
                jax.ShapeDtypeStruct((deep, half_cols), BF16),
            ],
            (place, own_gain, *[x for _, _, x in sources]),
            [SMEM, VMEM] + [ANY] * n_role,
            scratch=[
                pltpu.VMEM((n_role, rows, wide), BF16),
                pltpu.VMEM((deep, wide), F32),
                pltpu.SemaphoreType.DMA((n_role,)),
            ],
            limit=12,
        )

        forward = [(i, (i + 1) % n_group) for i in range(n_group)]
        rings = [[array] for array in held]
        for _ in range(1, n_group):
            for array in rings:
                array.append(lax.ppermute(array[-1], "group", forward))
        kv_parts, left_parts, right_parts = rings
        where = jnp.stack([(group - s) % n_group for s in range(n_group)]).astype(jnp.int32)

        own = tokens[0].T
        blocks = [(0, None, own)]
        bit = inner // 2
        while bit:
            if bit > 1 and split > 1 and len(blocks) == 1:
                piece = lax.dynamic_slice(own, (plane * part, 0), (part, block))
                piece, _ = lax.optimization_barrier((piece, packed[1]))
                piece = swap(piece, "role", n_role, bit)
                blocks.append((bit, 0, piece))
                for t in range(1, split):
                    after = [(i, (i + 1) % split) for i in range(split)]
                    piece = lax.ppermute(piece, "tensor", after)
                    blocks.append((bit, t, piece))
                last_token = blocks[1][2]
            else:
                blocks += [
                    (m ^ bit, t, swap(x, "role", n_role, bit))
                    for m, t, x in blocks
                ]
            bit //= 2

        positions = (ring * span + jnp.arange(span, dtype=jnp.int32)).astype(F32)
        frequency = jnp.exp(-jnp.log(150000.0) * jnp.arange(HALF, dtype=F32) / HALF)
        angle = frequency[:, None] * positions[None, :]
        turn = jnp.stack([jnp.cos(angle), jnp.sin(angle)])

        tile = math.gcd(span, 256)

        def rotated(vector, turn_ref, at):
            a, b = vector[:HALF], vector[HALF:]
            cosine, sine = turn_ref[0, :, at], turn_ref[1, :, at]
            return jnp.concatenate([a * cosine - b * sine, b * cosine + a * sine], axis=0)

        early = n_group - 1
        n_blocks = len(blocks)

        def early_body(at, where_ref, turn_ref, *refs):
            parts, refs = refs[:n_blocks], refs[n_blocks:]
            weight_refs, refs = refs[: n_group + 2 * early], refs[n_group + 2 * early :]
            kv_out, begun_out, scale_out, late_out, x, kvs, full, sems = refs
            pairs = [(ref, kvs.at[s]) for s, ref in enumerate(weight_refs[:n_group])]
            for s in range(early):
                for a in range(2):
                    lanes = pl.ds(a * half_cols, half_cols)
                    pairs.append((weight_refs[n_group + a * early + s], full.at[s, :, lanes]))
            for ref, (m, t, _) in zip(parts, blocks):
                start = pl.multiple_of((at[0] ^ m) * block, LANES)
                first_row = 0
                if t is not None:
                    first_row = pl.multiple_of(lax.rem(at[1] + split - t, split) * part, 16)
                target = x.at[pl.ds(first_row, ref.shape[0]), pl.ds(start, block)]
                pairs.append((ref, target))
            copies = fetch(pairs, sems)
            for copy in copies[:n_group]:
                copy.wait()
            for s in range(n_group):
                full[s, :, cols:] = jnp.zeros((deep, LANES), BF16)
                full[s, :kv_deep, cols : cols + HEAD_DIM] = kvs[s, :, :HEAD_DIM]
                full[s, kv_deep:, cols : cols + HEAD_DIM] = kvs[s, : deep - kv_deep, HEAD_DIM:]
            for copy in copies[n_group:]:
                copy.wait()
            spots = [pl.ds(pl.multiple_of(where_ref[s] * deep, 16), deep) for s in range(n_group)]
            late_out[...] = x[spots[early], :]
            for t in range(span // tile):
                lanes = slice(t * tile, (t + 1) * tile)
                squares = jnp.zeros((1, tile), F32)
                for s in range(n_group):
                    piece = x[s * deep : (s + 1) * deep, lanes].astype(F32)
                    squares = squares + jnp.sum(piece * piece, axis=0, keepdims=True)
                scale = lax.rsqrt(squares / width + 1e-05)
                scale_out[:, lanes] = scale
                total = contract(full[early, :, cols:], x[spots[early], lanes])[:HEAD_DIM]
                begun = None
                for s in range(early):
                    added = contract(full[s], x[spots[s], lanes])
                    total = total + added[cols : cols + HEAD_DIM]
                    begun = added[:cols] if begun is None else begun + added[:cols]
                begun_out[:, lanes] = begun
                total = total * scale
                turned = rotated(total, turn_ref, lanes)
                kv_out[:, lanes] = jnp.where(at[0] % 2 == 0, turned, total).astype(BF16)

        kv_mine, begun, scales, x_late = call(
            early_body,
            [
                jax.ShapeDtypeStruct((HEAD_DIM, span), BF16),
                jax.ShapeDtypeStruct((cols, span), F32),
                jax.ShapeDtypeStruct((1, span), F32),
                jax.ShapeDtypeStruct((deep, span), BF16),
            ],
            (
                place,
                where,
                turn,
                *[x for _, _, x in blocks],
                *kv_parts,
                *left_parts[:early],
                *right_parts[:early],
            ),
            [SMEM, SMEM, VMEM] + [ANY] * (n_blocks + n_group + 2 * early),
            scratch=[
                pltpu.VMEM((width, span), BF16),
                pltpu.VMEM((n_group, kv_deep, LANES), BF16),
                pltpu.VMEM((n_group, deep, wide), BF16),
                pltpu.SemaphoreType.DMA((n_blocks + n_group + 2 * early,)),
            ],
            flops=2 * width * (cols + HEAD_DIM) * span,
            limit=28,
        )
        if outer == 1:
            kv_pair = (kv_mine, swap(kv_mine, "role", n_role, 1))
            flip = mine % 2
        else:
            both = lax.all_gather(kv_mine, "role", axis=0).reshape(outer, inner, HEAD_DIM, span)

            def along(index):
                taken = lax.dynamic_index_in_dim(both, index, 1, keepdims=False)
                return jnp.swapaxes(taken, 0, 1).reshape(HEAD_DIM, seq)

            kv_pair = (along((mine // 2) * 2), along((mine // 2) * 2 + 1))
            flip = jnp.int32(0)

        def late_body(turn_ref, scale_ref, x_ref, begun_ref, left_ref, right_ref, out_ref):
            weight = jnp.concatenate([left_ref[...], right_ref[...]], axis=1)
            for t in range(span // tile):
                lanes = slice(t * tile, (t + 1) * tile)
                total = begun_ref[:, lanes] + contract(weight, x_ref[:, lanes])
                total = total * (scale_ref[:, lanes] * 0.125)
                for h in range(heads):
                    here = slice(h * HEAD_DIM, (h + 1) * HEAD_DIM)
                    out_ref[here, lanes] = rotated(total[here], turn_ref, lanes).astype(BF16)

        queries = call(
            late_body,
            jax.ShapeDtypeStruct((cols, span), BF16),
            (turn, scales, x_late, begun, left_parts[early], right_parts[early]),
            [VMEM] * 6,
            flops=2 * deep * cols * span,
            limit=12,
        )

        shared = out_weight.T
        if split > 1:
            shared, _ = lax.optimization_barrier((shared, last_token))
        gathered = [(0, segments)]
        weights_out = [(0, shared)]
        bit = n_role // 2
        while bit:
            gathered += [(m ^ bit, swap(x, "role", n_role, bit)) for m, x in gathered]
            weights_out += [(m ^ bit, swap(x, "role", n_role, bit)) for m, x in weights_out]
            bit //= 2
        docs = jnp.zeros((n_role, block), jnp.int32)
        for m, x in gathered:
            docs = lax.dynamic_update_slice(docs, x, (role ^ m, 0))
        docs = docs.reshape(seq)
        own_docs = lax.dynamic_slice(docs, (ring * span,), (span,))
        first = jnp.sum((docs[:, None] < own_docs[None, :]).astype(jnp.int32), axis=0)
        lowest = first[::block] // block
        first = first[None, :]
        sink_terms = jnp.exp(sinks)
        turns = jnp.stack([mine, flip, ring]).astype(jnp.int32)

        copies_out = n_tensor if outer == 1 else 1

        def attend_body(
            at, lowest_ref, sink_ref, first_ref, q_ref, a_ref, b_ref, out_ref, k_ref, v_ref, half
        ):
            base = half * half_heads
            k_ref[...] = jnp.where(at[1] == 0, a_ref[...], b_ref[...])
            v_ref[...] = jnp.where(at[1] == 0, b_ref[...], a_ref[...])
            for qb in range(inner):
                lanes = slice(qb * block, (qb + 1) * block)
                start = first_ref[:, lanes]
                last = at[2] * inner + qb
                pos = last * block + lax.broadcasted_iota(jnp.int32, (1, block), 1)
                qs = [
                    q_ref[(base + h) * HEAD_DIM : (base + h + 1) * HEAD_DIM, lanes]
                    for h in range(half_heads)
                ]

                def advance(kb, carry):
                    at_key = pl.multiple_of(kb * block, LANES)
                    k = k_ref[:, pl.ds(at_key, block)]
                    v = v_ref[:, pl.ds(at_key, block)]
                    index = kb * block + lax.broadcasted_iota(jnp.int32, (block, block), 0)
                    allowed = (index >= start) & (index <= pos)
                    after = []
                    for h in range(half_heads):
                        total, summed = carry[h]
                        weight = jnp.where(allowed, jnp.exp(contract(k, qs[h])), 0.0)
                        total = total + jnp.sum(weight, axis=0, keepdims=True)
                        summed = summed + jnp.dot(
                            v, weight.astype(BF16), preferred_element_type=F32
                        )
                        after.append((total, summed))
                    return tuple(after)

                zero = (jnp.zeros((1, block), F32), jnp.zeros((HEAD_DIM, block), F32))
                done = lax.fori_loop(lowest_ref[qb], last + 1, advance, (zero,) * half_heads)
                for h in range(half_heads):
                    total, summed = done[h]
                    total = total + sink_ref[at[0] * heads + base + h]
                    here = slice(h * HEAD_DIM, (h + 1) * HEAD_DIM)
                    value = (summed / total).astype(BF16)
                    for copy in range(copies_out):
                        out_ref[copy * inner + qb, here, :] = value

        def attend(half):
            def body(*refs):
                attend_body(*refs, half)

            return call(
                body,
                jax.ShapeDtypeStruct((copies_out * inner, half_cols, block), BF16),
                (turns, lowest, sink_terms, first, queries, *kv_pair),
                [SMEM, SMEM, SMEM] + [VMEM] * 4,
                scratch=[pltpu.VMEM((HEAD_DIM, seq), BF16)] * 2,
                flops=half_heads * 4 * HEAD_DIM * span * seq // 2,
            )

        def exchange(context):
            if outer == 1:
                return lax.all_to_all(context, ("tensor", "role"), 0, 0, tiled=True)
            pieces_in = []
            for k in range(inner):
                piece = lax.dynamic_index_in_dim(context, mine ^ k, 0, keepdims=False)
                pieces_in.append(swap(piece, "role", n_role, k) if k else piece)
            stacked = jnp.stack(pieces_in)
            ordered = jnp.stack(
                [lax.dynamic_index_in_dim(stacked, mine ^ i, 0, keepdims=False) for i in range(inner)]
            )
            every = lax.all_gather(ordered, "tensor", axis=0)
            return every.reshape(n_tensor * inner, half_cols, block)

        context = [exchange(attend(half)) for half in range(2)]

        table = jnp.stack([role ^ m for m, _ in weights_out]).astype(jnp.int32)

        units = out_rows // (2 * half_cols)
        phased = units * 2 * half_cols == out_rows
        lists = [x for _, x in weights_out]

        def dots(table_ref, weight, source):
            total = None
            for k in range(n_role):
                added = jnp.dot(weight(k), source(table_ref[k]), preferred_element_type=F32)
                total = added if total is None else total + added
            return total

        def mix(half, begun_mix):
            def body(table_ref, context_ref, *refs):
                if half:
                    before, refs = refs[0], refs[1:]
                hbm, (out_ref, held_ref, sems) = refs[:n_role], refs[n_role:]
                pairs = []
                for k in range(n_role):
                    for u in range(units):
                        there = pl.ds((2 * u + half) * half_cols, half_cols)
                        here = pl.ds(u * half_cols, half_cols)
                        pairs.append((hbm[k].at[:, there], held_ref.at[k, :, here]))
                for copy in fetch(pairs, sems):
                    copy.wait()

                def source(b):
                    return context_ref[pl.ds(b * units, units)].reshape(units * half_cols, block)

                total = dots(table_ref, lambda k: held_ref[k], source)
                out_ref[...] = (total + before[...]).astype(BF16) if half else total

            return call(
                body,
                jax.ShapeDtypeStruct((out_cols, block), BF16 if half else F32),
                (table, context[half], *([begun_mix] if half else []), *lists),
                [SMEM, VMEM] + [VMEM] * half + [ANY] * n_role,
                scratch=[
                    pltpu.VMEM((n_role, out_cols, units * half_cols), BF16),
                    pltpu.SemaphoreType.DMA((n_role * units,)),
                ],
                flops=n_role * out_rows * out_cols * block,
                limit=16,
            )

        def out_body(table_ref, one_ref, two_ref, *refs):
            weights, out_ref, nat = refs[:n_role], refs[n_role], refs[n_role + 1]
            for i in range(n_tensor * inner):
                nat[i * cols : i * cols + half_cols] = one_ref[i]
                nat[i * cols + half_cols : (i + 1) * cols] = two_ref[i]

            def source(b):
                return nat[pl.ds(pl.multiple_of(b * out_rows, 16), out_rows), :]

            total = dots(table_ref, lambda k: weights[k][...], source)
            out_ref[...] = total.astype(BF16)

        if phased:
            mixed = mix(1, mix(0, None))
        else:
            mixed = call(
                out_body,
                jax.ShapeDtypeStruct((out_cols, block), BF16),
                (table, *context, *lists),
                [SMEM] + [VMEM] * (2 + n_role),
                scratch=[pltpu.VMEM((n_role * out_rows, block), BF16)],
                flops=2 * n_role * out_rows * out_cols * block,
                limit=20,
            )
        return mixed.T[None]

    return on_device


def solution(mesh):
    placed = (
        P("group", "role", None),
        P(),
        P(("group", "role"), "tensor"),
        P(("group", "role"), "tensor"),
        P("role", "tensor"),
        P("tensor"),
        P("group", "role"),
    )
    return jax.shard_map(
        make_step(mesh),
        mesh=mesh,
        in_specs=placed,
        out_specs=P("group", "role", "tensor"),
        check_vma=False,
    )
```

```python
import math

import jax
import jax.numpy as jnp
from jax import lax
from jax.experimental import pallas as pl
from jax.experimental.pallas import tpu as pltpu
from jax.sharding import PartitionSpec as P


HEAD_DIM = 64
HALF = HEAD_DIM // 2
LANES = 128
BF16 = jnp.bfloat16
F32 = jnp.float32


VMEM = pl.BlockSpec(memory_space=pltpu.VMEM)
SMEM = pl.BlockSpec(memory_space=pltpu.SMEM)
HBM = pl.BlockSpec(memory_space=pltpu.HBM)


def call(body, outs, args, specs, scratch=(), flops=0, moved=0, limit=16):
    return pl.pallas_call(
        body,
        out_shape=outs,
        in_specs=specs,
        out_specs=jax.tree.map(lambda _: VMEM, outs),
        scratch_shapes=scratch,
        compiler_params=pltpu.CompilerParams(vmem_limit_bytes=limit << 20),
        cost_estimate=pl.CostEstimate(flops=flops, bytes_accessed=moved, transcendentals=0),
    )(*args)


def swap(array, axis, size, mask):
    return lax.ppermute(array, axis, [(i, i ^ mask) for i in range(size)])


def fetch(pairs, sems):
    copies = [pltpu.make_async_copy(a, b, sems.at[i]) for i, (a, b) in enumerate(pairs)]
    for copy in copies:
        copy.start()
    return copies


def contract(left, right):
    return lax.dot_general(left, right, (((0,), (0,)), ((), ())), preferred_element_type=F32)


def make_step(mesh):
    n_group, n_tensor, n_role = mesh.shape["group"], mesh.shape["tensor"], mesh.shape["role"]

    def on_device(tokens, gain, q_weight, kv_weight, out_weight, sinks, segments):
        block = tokens.shape[1]
        width = tokens.shape[2]
        rows, q_cols = q_weight.shape
        pair_cols = kv_weight.shape[1]
        pairs = pair_cols // (2 * HEAD_DIM)
        inner = 2 * pairs
        outer = n_role // inner
        cols = q_cols // inner
        heads = cols // HEAD_DIM
        half_cols = cols // 2
        half_heads = heads // 2
        span = inner * block
        seq = n_role * block
        out_rows, out_cols = out_weight.shape
        split = n_tensor if inner > 2 and width % (16 * n_tensor) == 0 else 1
        part = width // split

        group = lax.axis_index("group")
        plane = lax.axis_index("tensor")
        role = lax.axis_index("role")
        mine = role % inner
        ring = role // inner
        place = jnp.stack([mine, plane, ring]).astype(jnp.int32)

        wide = cols + LANES

        own = tokens[0].T
        chunks = 2 if split > 1 and part % 32 == 0 else split - 1
        chunk = part // max(chunks, 1)

        def pack_body(at, q_hbm, kv_hbm, x_hbm, *outs):
            outs, halves, (q_ref, kv_ref, sems) = (
                outs[:inner],
                outs[inner : inner + chunks],
                outs[inner + chunks :],
            )
            pairs = [(q_hbm, q_ref), (kv_hbm, kv_ref)]
            for i, half_ref in enumerate(halves):
                first_row = pl.multiple_of(at[1] * part + i * chunk, 16)
                pairs.append((x_hbm.at[pl.ds(first_row, chunk)], half_ref))
            copies = fetch(pairs, sems)
            for copy in copies[:2]:
                copy.wait()
            for k in range(inner):
                target = at[0] ^ k
                outs[k][:, :cols] = q_ref[:, pl.ds(pl.multiple_of(target * cols, LANES), cols)]
                pair = kv_ref[:, pl.ds(pl.multiple_of((target // 2) * LANES, LANES), LANES)]
                chosen = jnp.where(target % 2 == 0, pair[:, :HEAD_DIM], pair[:, HEAD_DIM:])
                outs[k][:, cols : cols + HEAD_DIM] = chosen
                outs[k][:, cols + HEAD_DIM :] = jnp.zeros((rows, HEAD_DIM), BF16)
            for copy in copies[2:]:
                copy.wait()

        packed = call(
            pack_body,
            [jax.ShapeDtypeStruct((rows, wide), BF16)] * inner
            + [jax.ShapeDtypeStruct((chunk, block), BF16)] * chunks,
            (place, q_weight, kv_weight, own),
            [SMEM, HBM, HBM, HBM],
            scratch=[
                pltpu.VMEM(q_weight.shape, BF16),
                pltpu.VMEM(kv_weight.shape, BF16),
                pltpu.SemaphoreType.DMA((2 + chunks,)),
            ],
            limit=60,
        )
        got = [packed[0]] + [swap(packed[k], "role", n_role, k) for k in range(1, inner)]
        sources = [(0, k, x) for k, x in enumerate(got)]
        for o in range(1, outer):
            ahead = [(i, (i + o * inner) % n_role) for i in range(n_role)]
            sources += [(o, k, lax.ppermute(x, "role", ahead)) for k, x in enumerate(got)]

        deep = n_role * rows
        kv_deep = -(-deep // 32) * 16
        own_gain = lax.dynamic_slice(gain, (group * deep,), (deep,))
        own_gain = jnp.broadcast_to(own_gain[:, None], (deep, LANES))

        def stack_body(at, gain_ref, *refs):
            kv_out, left_out, right_out, one, two, sems = refs[n_role:]
            pairs = []
            for ref, (o, k, _) in zip(refs[:n_role], sources):
                spot = lax.rem(at[2] + outer - o, outer) * inner + (at[0] ^ k)
                pairs.append((ref, one.at[spot]))
            for copy in fetch(pairs, sems):
                copy.wait()
            for p in range(n_role):
                two[p * rows : (p + 1) * rows, :] = one[p].astype(F32)
            for out_ref, c in ((left_out, 0), (right_out, half_cols)):
                for lane in range(0, half_cols, LANES):
                    here = slice(lane, lane + LANES)
                    there = slice(c + lane, c + lane + LANES)
                    out_ref[:, here] = (two[:, there] * gain_ref[...]).astype(BF16)
            kv = (two[:, cols:] * gain_ref[...])[:, :HEAD_DIM].astype(BF16)
            kv_out[...] = jnp.zeros_like(kv_out)
            kv_out[:, :HEAD_DIM] = kv[:kv_deep]
            kv_out[: deep - kv_deep, HEAD_DIM:] = kv[kv_deep:]

        held = call(
            stack_body,
            [
                jax.ShapeDtypeStruct((kv_deep, LANES), BF16),
                jax.ShapeDtypeStruct((deep, half_cols), BF16),
                jax.ShapeDtypeStruct((deep, half_cols), BF16),
            ],
            (place, own_gain, *[x for _, _, x in sources]),
            [SMEM, VMEM] + [HBM] * n_role,
            scratch=[
                pltpu.VMEM((n_role, rows, wide), BF16),
                pltpu.VMEM((deep, wide), F32),
                pltpu.SemaphoreType.DMA((n_role,)),
            ],
            limit=60,
        )

        forward = [(i, (i + 1) % n_group) for i in range(n_group)]
        rings = [[array] for array in held]
        for _ in range(1, n_group):
            for array in rings:
                array.append(lax.ppermute(array[-1], "group", forward))
        kv_parts, left_parts, right_parts = rings
        where = jnp.stack([(group - s) % n_group for s in range(n_group)]).astype(jnp.int32)

        blocks = [(0, None, 0, own)]
        bit = inner // 2
        last_token = None
        while bit:
            if bit > 1 and split > 1 and len(blocks) == 1:
                after = [(i, (i + 1) % split) for i in range(split)]
                for i in range(chunks):
                    piece = swap(packed[inner + i], "role", n_role, bit)
                    last_token = piece
                    blocks.append((bit, 0, i * chunk, piece))
                    for t in range(1, split):
                        piece = lax.ppermute(piece, "tensor", after)
                        blocks.append((bit, t, i * chunk, piece))
            else:
                blocks += [
                    (
                        m ^ bit,
                        t,
                        r,
                        swap(x, "role", n_role, bit),
                    )
                    for m, t, r, x in blocks
                ]
            bit //= 2

        positions = (ring * span + jnp.arange(span, dtype=jnp.int32)).astype(F32)
        frequency = jnp.exp(-jnp.log(150000.0) * jnp.arange(HALF, dtype=F32) / HALF)
        angle = frequency[:, None] * positions[None, :]
        turn = jnp.stack([jnp.cos(angle), jnp.sin(angle)])

        tile = math.gcd(span, 256)

        def rotated(vector, turn_ref, at):
            a, b = vector[:HALF], vector[HALF:]
            cosine, sine = turn_ref[0, :, at], turn_ref[1, :, at]
            return jnp.concatenate([a * cosine - b * sine, b * cosine + a * sine], axis=0)

        early = n_group - 1
        n_blocks = len(blocks)

        def early_body(at, where_ref, turn_ref, *refs):
            parts, refs = refs[:n_blocks], refs[n_blocks:]
            weight_refs, refs = refs[: n_group + 2 * early], refs[n_group + 2 * early :]
            kv_out, begun_out, scale_out, late_out, x, kvs, full, sems = refs
            pairs = [(ref, kvs.at[s]) for s, ref in enumerate(weight_refs[:n_group])]
            for s in range(early):
                for a in range(2):
                    lanes = pl.ds(a * half_cols, half_cols)
                    pairs.append((weight_refs[n_group + a * early + s], full.at[s, :, lanes]))
            for ref, (m, t, r, _) in zip(parts, blocks):
                start = pl.multiple_of((at[0] ^ m) * block, LANES)
                first_row = 0
                if t is not None:
                    first_row = pl.multiple_of(lax.rem(at[1] + split - t, split) * part + r, 16)
                target = x.at[pl.ds(first_row, ref.shape[0]), pl.ds(start, block)]
                pairs.append((ref, target))
            copies = fetch(pairs, sems)
            for copy in copies[:n_group]:
                copy.wait()
            for s in range(n_group):
                full[s, :, cols:] = jnp.zeros((deep, LANES), BF16)
                full[s, :kv_deep, cols : cols + HEAD_DIM] = kvs[s, :, :HEAD_DIM]
                full[s, kv_deep:, cols : cols + HEAD_DIM] = kvs[s, : deep - kv_deep, HEAD_DIM:]
            for copy in copies[n_group:]:
                copy.wait()
            spots = [pl.ds(pl.multiple_of(where_ref[s] * deep, 16), deep) for s in range(n_group)]
            late_out[...] = x[spots[early], :]
            for t in range(span // tile):
                lanes = slice(t * tile, (t + 1) * tile)
                squares = jnp.zeros((1, tile), F32)
                for s in range(n_group):
                    piece = x[s * deep : (s + 1) * deep, lanes].astype(F32)
                    squares = squares + jnp.sum(piece * piece, axis=0, keepdims=True)
                scale = lax.rsqrt(squares / width + 1e-05)
                scale_out[:, lanes] = scale
                total = contract(full[early, :, cols:], x[spots[early], lanes])[:HEAD_DIM]
                begun = None
                for s in range(early):
                    added = contract(full[s], x[spots[s], lanes])
                    total = total + added[cols : cols + HEAD_DIM]
                    begun = added[:cols] if begun is None else begun + added[:cols]
                begun_out[:, lanes] = begun
                total = total * scale
                turned = rotated(total, turn_ref, lanes)
                kv_out[:, lanes] = jnp.where(at[0] % 2 == 0, turned, total).astype(BF16)

        kv_mine, begun, scales, x_late = call(
            early_body,
            [
                jax.ShapeDtypeStruct((HEAD_DIM, span), BF16),
                jax.ShapeDtypeStruct((cols, span), F32),
                jax.ShapeDtypeStruct((1, span), F32),
                jax.ShapeDtypeStruct((deep, span), BF16),
            ],
            (
                place,
                where,
                turn,
                *[x for _, _, _, x in blocks],
                *kv_parts,
                *left_parts[:early],
                *right_parts[:early],
            ),
            [SMEM, SMEM, VMEM] + [HBM] * (n_blocks + n_group + 2 * early),
            scratch=[
                pltpu.VMEM((width, span), BF16),
                pltpu.VMEM((n_group, kv_deep, LANES), BF16),
                pltpu.VMEM((n_group, deep, wide), BF16),
                pltpu.SemaphoreType.DMA((n_blocks + n_group + 2 * early,)),
            ],
            flops=2 * width * (cols + HEAD_DIM) * span,
            limit=28,
        )
        if outer == 1:
            kv_pair = (kv_mine, swap(kv_mine, "role", n_role, 1))
            flip = mine % 2
        else:
            both = lax.all_gather(kv_mine, "role", axis=0).reshape(outer, inner, HEAD_DIM, span)

            def along(index):
                taken = lax.dynamic_index_in_dim(both, index, 1, keepdims=False)
                return jnp.swapaxes(taken, 0, 1).reshape(HEAD_DIM, seq)

            kv_pair = (along((mine // 2) * 2), along((mine // 2) * 2 + 1))
            flip = jnp.int32(0)

        def late_body(turn_ref, scale_ref, x_ref, begun_ref, left_ref, right_ref, out_ref):
            weight = jnp.concatenate([left_ref[...], right_ref[...]], axis=1)
            for t in range(span // tile):
                lanes = slice(t * tile, (t + 1) * tile)
                total = begun_ref[:, lanes] + contract(weight, x_ref[:, lanes])
                total = total * (scale_ref[:, lanes] * 0.125)
                for h in range(heads):
                    here = slice(h * HEAD_DIM, (h + 1) * HEAD_DIM)
                    out_ref[here, lanes] = rotated(total[here], turn_ref, lanes).astype(BF16)

        queries = call(
            late_body,
            jax.ShapeDtypeStruct((cols, span), BF16),
            (turn, scales, x_late, begun, left_parts[early], right_parts[early]),
            [VMEM] * 6,
            flops=2 * deep * cols * span,
            limit=12,
        )

        shared = out_weight.T
        if split > 1:
            shared, _ = lax.optimization_barrier((shared, last_token))
        gathered = [(0, segments)]
        weights_out = [(0, shared)]
        bit = n_role // 2
        while bit:
            gathered += [(m ^ bit, swap(x, "role", n_role, bit)) for m, x in gathered]
            weights_out += [(m ^ bit, swap(x, "role", n_role, bit)) for m, x in weights_out]
            bit //= 2
        docs = jnp.zeros((n_role, block), jnp.int32)
        for m, x in gathered:
            docs = lax.dynamic_update_slice(docs, x, (role ^ m, 0))
        docs = docs.reshape(seq)
        own_docs = lax.dynamic_slice(docs, (ring * span,), (span,))
        first = jnp.sum((docs[:, None] < own_docs[None, :]).astype(jnp.int32), axis=0)
        lowest = first[::block] // block
        first = first[None, :]
        sink_terms = jnp.exp(sinks)
        turns = jnp.stack([mine, flip, ring]).astype(jnp.int32)

        copies_out = n_tensor if outer == 1 else 1

        def attend_body(
            at, lowest_ref, sink_ref, first_ref, q_ref, a_ref, b_ref, out_ref, k_ref, v_ref, half
        ):
            base = half * half_heads
            k_ref[...] = jnp.where(at[1] == 0, a_ref[...], b_ref[...])
            v_ref[...] = jnp.where(at[1] == 0, b_ref[...], a_ref[...])
            for qb in range(inner):
                lanes = slice(qb * block, (qb + 1) * block)
                start = first_ref[:, lanes]
                last = at[2] * inner + qb
                pos = last * block + lax.broadcasted_iota(jnp.int32, (1, block), 1)
                qs = [
                    q_ref[(base + h) * HEAD_DIM : (base + h + 1) * HEAD_DIM, lanes]
                    for h in range(half_heads)
                ]

                def advance(kb, carry):
                    at_key = pl.multiple_of(kb * block, LANES)
                    k = k_ref[:, pl.ds(at_key, block)]
                    v = v_ref[:, pl.ds(at_key, block)]
                    index = kb * block + lax.broadcasted_iota(jnp.int32, (block, block), 0)
                    allowed = (index >= start) & (index <= pos)
                    after = []
                    for h in range(half_heads):
                        total, summed = carry[h]
                        weight = jnp.where(allowed, jnp.exp(contract(k, qs[h])), 0.0)
                        total = total + jnp.sum(weight, axis=0, keepdims=True)
                        summed = summed + jnp.dot(
                            v, weight.astype(BF16), preferred_element_type=F32
                        )
                        after.append((total, summed))
                    return tuple(after)

                zero = (jnp.zeros((1, block), F32), jnp.zeros((HEAD_DIM, block), F32))
                done = lax.fori_loop(lowest_ref[qb], last + 1, advance, (zero,) * half_heads)
                for h in range(half_heads):
                    total, summed = done[h]
                    total = total + sink_ref[at[0] * heads + base + h]
                    here = slice(h * HEAD_DIM, (h + 1) * HEAD_DIM)
                    value = (summed / total).astype(BF16)
                    for copy in range(copies_out):
                        out_ref[copy * inner + qb, here, :] = value

        def attend(half):
            def body(*refs):
                attend_body(*refs, half)

            return call(
                body,
                jax.ShapeDtypeStruct((copies_out * inner, half_cols, block), BF16),
                (turns, lowest, sink_terms, first, queries, *kv_pair),
                [SMEM, SMEM, SMEM] + [VMEM] * 4,
                scratch=[pltpu.VMEM((HEAD_DIM, seq), BF16)] * 2,
                flops=half_heads * 4 * HEAD_DIM * span * seq // 2,
            )

        def exchange(context):
            if outer == 1:
                return lax.all_to_all(context, ("tensor", "role"), 0, 0, tiled=True)
            pieces_in = []
            for k in range(inner):
                piece = lax.dynamic_index_in_dim(context, mine ^ k, 0, keepdims=False)
                pieces_in.append(swap(piece, "role", n_role, k) if k else piece)
            stacked = jnp.stack(pieces_in)
            ordered = jnp.stack(
                [lax.dynamic_index_in_dim(stacked, mine ^ i, 0, keepdims=False) for i in range(inner)]
            )
            every = lax.all_gather(ordered, "tensor", axis=0)
            return every.reshape(n_tensor * inner, half_cols, block)

        context = [exchange(attend(half)) for half in range(2)]

        table = jnp.stack([role ^ m for m, _ in weights_out]).astype(jnp.int32)

        units = out_rows // (2 * half_cols)
        phased = units * 2 * half_cols == out_rows
        lists = [x for _, x in weights_out]

        def dots(table_ref, weight, source):
            total = None
            for k in range(n_role):
                added = jnp.dot(weight(k), source(table_ref[k]), preferred_element_type=F32)
                total = added if total is None else total + added
            return total

        def mix(half, begun_mix):
            def body(table_ref, context_ref, *refs):
                if half:
                    before, refs = refs[0], refs[1:]
                hbm, (out_ref, held_ref, sems) = refs[:n_role], refs[n_role:]
                pairs = []
                for k in range(n_role):
                    for u in range(units):
                        there = pl.ds((2 * u + half) * half_cols, half_cols)
                        here = pl.ds(u * half_cols, half_cols)
                        pairs.append((hbm[k].at[:, there], held_ref.at[k, :, here]))
                for copy in fetch(pairs, sems):
                    copy.wait()

                def source(b):
                    return context_ref[pl.ds(b * units, units)].reshape(units * half_cols, block)

                total = dots(table_ref, lambda k: held_ref[k], source)
                out_ref[...] = (total + before[...]).astype(BF16) if half else total

            return call(
                body,
                jax.ShapeDtypeStruct((out_cols, block), BF16 if half else F32),
                (table, context[half], *([begun_mix] if half else []), *lists),
                [SMEM, VMEM] + [VMEM] * half + [HBM] * n_role,
                scratch=[
                    pltpu.VMEM((n_role, out_cols, units * half_cols), BF16),
                    pltpu.SemaphoreType.DMA((n_role * units,)),
                ],
                flops=n_role * out_rows * out_cols * block,
                limit=16,
            )

        def out_body(table_ref, one_ref, two_ref, *refs):
            weights, out_ref, nat = refs[:n_role], refs[n_role], refs[n_role + 1]
            for i in range(n_tensor * inner):
                nat[i * cols : i * cols + half_cols] = one_ref[i]
                nat[i * cols + half_cols : (i + 1) * cols] = two_ref[i]

            def source(b):
                return nat[pl.ds(pl.multiple_of(b * out_rows, 16), out_rows), :]

            total = dots(table_ref, lambda k: weights[k][...], source)
            out_ref[...] = total.astype(BF16)

        if phased:
            mixed = mix(1, mix(0, None))
        else:
            mixed = call(
                out_body,
                jax.ShapeDtypeStruct((out_cols, block), BF16),
                (table, *context, *lists),
                [SMEM] + [VMEM] * (2 + n_role),
                scratch=[pltpu.VMEM((n_role * out_rows, block), BF16)],
                flops=2 * n_role * out_rows * out_cols * block,
                limit=20,
            )
        return mixed.T[None]

    return on_device


def solution(mesh):
    placed = (
        P("group", "role", None),
        P(),
        P(("group", "role"), "tensor"),
        P(("group", "role"), "tensor"),
        P("role", "tensor"),
        P("tensor"),
        P("group", "role"),
    )
    return jax.shard_map(
        make_step(mesh),
        mesh=mesh,
        in_specs=placed,
        out_specs=P("group", "role", "tensor"),
        check_vma=False,
    )
```

```python
import jax
import jax.numpy as jnp
from jax import lax
from jax.experimental import pallas as pl
from jax.experimental.pallas import tpu as pltpu
from jax.sharding import PartitionSpec as P


HEAD_DIM = 64
HALF = HEAD_DIM // 2
LANES = 128
BF16 = jnp.bfloat16
F32 = jnp.float32


VMEM = pl.BlockSpec(memory_space=pltpu.VMEM)
SMEM = pl.BlockSpec(memory_space=pltpu.SMEM)
HBM = pl.BlockSpec(memory_space=pltpu.HBM)


def call(body, outs, args, specs, scratch=(), flops=0, moved=0):
    return pl.pallas_call(
        body,
        out_shape=outs,
        in_specs=specs,
        out_specs=jax.tree.map(lambda _: VMEM, outs),
        scratch_shapes=scratch,
        compiler_params=pltpu.CompilerParams(vmem_limit_bytes=60 << 20),
        cost_estimate=pl.CostEstimate(flops=flops, bytes_accessed=moved, transcendentals=0),
    )(*args)


def swap(array, axis, size, mask):
    return lax.ppermute(array, axis, [(i, i ^ mask) for i in range(size)])


def fetch(pairs, sems):
    copies = [pltpu.make_async_copy(a, b, sems.at[i]) for i, (a, b) in enumerate(pairs)]
    for copy in copies:
        copy.start()
    return copies


def contract(left, right):
    return lax.dot_general(left, right, (((0,), (0,)), ((), ())), preferred_element_type=F32)


def make_step(mesh):
    n_group, n_tensor, n_role = mesh.shape["group"], mesh.shape["tensor"], mesh.shape["role"]

    def on_device(tokens, gain, q_weight, kv_weight, out_weight, sinks, segments):
        block = tokens.shape[1]
        width = tokens.shape[2]
        rows, q_cols = q_weight.shape
        pair_cols = kv_weight.shape[1]
        pairs = pair_cols // (2 * HEAD_DIM)
        inner = 2 * pairs
        outer = n_role // inner
        cols = q_cols // inner
        heads = cols // HEAD_DIM
        half_cols = cols // 2
        half_heads = heads // 2
        span = inner * block
        seq = n_role * block
        out_rows, out_cols = out_weight.shape
        split = n_tensor if inner > 2 and width % (16 * n_tensor) == 0 else 1
        part = width // split

        group = lax.axis_index("group")
        plane = lax.axis_index("tensor")
        role = lax.axis_index("role")
        mine = role % inner
        ring = role // inner
        place = jnp.stack([mine, plane, ring]).astype(jnp.int32)

        wide = cols + LANES

        own = tokens[0].T
        chunks = 2 if split > 1 and part % 32 == 0 else split - 1
        chunk = part // max(chunks, 1)

        def pack_body(at, q_hbm, kv_hbm, x_hbm, *outs):
            outs, halves, (q_ref, kv_ref, sems) = (
                outs[:inner],
                outs[inner : inner + chunks],
                outs[inner + chunks :],
            )
            pairs = [(q_hbm, q_ref), (kv_hbm, kv_ref)]
            for i, half_ref in enumerate(halves):
                first_row = pl.multiple_of(at[1] * part + i * chunk, 16)
                pairs.append((x_hbm.at[pl.ds(first_row, chunk)], half_ref))
            copies = fetch(pairs, sems)
            for copy in copies[:2]:
                copy.wait()
            for k in range(inner):
                target = at[0] ^ k
                outs[k][:, :cols] = q_ref[:, pl.ds(pl.multiple_of(target * cols, LANES), cols)]
                pair = kv_ref[:, pl.ds(pl.multiple_of((target // 2) * LANES, LANES), LANES)]
                chosen = jnp.where(target % 2 == 0, pair[:, :HEAD_DIM], pair[:, HEAD_DIM:])
                outs[k][:, cols : cols + HEAD_DIM] = chosen
                outs[k][:, cols + HEAD_DIM :] = jnp.zeros((rows, HEAD_DIM), BF16)
            for copy in copies[2:]:
                copy.wait()

        packed = call(
            pack_body,
            [jax.ShapeDtypeStruct((rows, wide), BF16)] * inner
            + [jax.ShapeDtypeStruct((chunk, block), BF16)] * chunks,
            (place, q_weight, kv_weight, own),
            [SMEM, HBM, HBM, HBM],
            scratch=[
                pltpu.VMEM(q_weight.shape, BF16),
                pltpu.VMEM(kv_weight.shape, BF16),
                pltpu.SemaphoreType.DMA((2 + chunks,)),
            ],
        )
        deep = n_role * rows
        kv_deep = -(-deep // 32) * 16

        def stacked(got, source_group):
            sources = [(0, k, x) for k, x in enumerate(got)]
            for o in range(1, outer):
                ahead = [(i, (i + o * inner) % n_role) for i in range(n_role)]
                sources += [(o, k, lax.ppermute(x, "role", ahead)) for k, x in enumerate(got)]
            rows_gain = lax.dynamic_slice(gain, (source_group * deep,), (deep,))
            rows_gain = jnp.broadcast_to(rows_gain[:, None], (deep, LANES))

            def stack_body(at, gain_ref, *refs):
                kv_out, left_out, right_out, one, two, sems = refs[n_role:]
                pairs = []
                for ref, (o, k, _) in zip(refs[:n_role], sources):
                    spot = lax.rem(at[2] + outer - o, outer) * inner + (at[0] ^ k)
                    pairs.append((ref, one.at[spot]))
                for copy in fetch(pairs, sems):
                    copy.wait()
                for p in range(n_role):
                    two[p * rows : (p + 1) * rows, :] = one[p].astype(F32)
                for out_ref, c in ((left_out, 0), (right_out, half_cols)):
                    for lane in range(0, half_cols, LANES):
                        here = slice(lane, lane + LANES)
                        there = slice(c + lane, c + lane + LANES)
                        out_ref[:, here] = (two[:, there] * gain_ref[...]).astype(BF16)
                kv = (two[:, cols:] * gain_ref[...])[:, :HEAD_DIM].astype(BF16)
                kv_out[...] = jnp.zeros_like(kv_out)
                kv_out[:, :HEAD_DIM] = kv[:kv_deep]
                kv_out[: deep - kv_deep, HEAD_DIM:] = kv[kv_deep:]

            return call(
                stack_body,
                [
                    jax.ShapeDtypeStruct((kv_deep, LANES), BF16),
                    jax.ShapeDtypeStruct((deep, half_cols), BF16),
                    jax.ShapeDtypeStruct((deep, half_cols), BF16),
                ],
                (place, rows_gain, *[x for _, _, x in sources]),
                [SMEM, VMEM] + [HBM] * n_role,
                scratch=[
                    pltpu.VMEM((n_role, rows, wide), BF16),
                    pltpu.VMEM((deep, wide), F32),
                    pltpu.SemaphoreType.DMA((n_role,)),
                ],
            )

        forward = [(i, (i + 1) % n_group) for i in range(n_group)]
        neighbours = []
        for k in range(inner):
            pairs = [
                (g * n_role + r, (g + 1) % n_group * n_role + (r ^ k))
                for g in range(n_group)
                for r in range(n_role)
            ]
            neighbours.append(lax.ppermute(packed[k], ("group", "role"), pairs))
        direct = stacked(neighbours, (group - 1) % n_group)
        near = [packed[0]] + [swap(packed[k], "role", n_role, k) for k in range(1, inner)]
        held = stacked(near, group)
        rings = [[x, y] for x, y in zip(held, direct)]
        for _ in range(2, n_group):
            for array in rings:
                array.append(lax.ppermute(array[-1], "group", forward))
        kv_parts, left_parts, right_parts = [array[:n_group] for array in rings]
        where = jnp.stack([(group - s) % n_group for s in range(n_group)]).astype(jnp.int32)

        blocks = [(0, None, 0, own)]
        bit = inner // 2
        last_token = None
        while bit:
            if bit > 1 and split > 1 and len(blocks) == 1:
                after = [(i, (i + 1) % split) for i in range(split)]
                for i in range(chunks):
                    piece = swap(packed[inner + i], "role", n_role, bit)
                    last_token = piece
                    blocks.append((bit, 0, i * chunk, piece))
                    for t in range(1, split):
                        piece = lax.ppermute(piece, "tensor", after)
                        blocks.append((bit, t, i * chunk, piece))
            else:
                blocks += [
                    (
                        m ^ bit,
                        t,
                        r,
                        swap(x, "role", n_role, bit),
                    )
                    for m, t, r, x in blocks
                ]
            bit //= 2

        positions = (ring * span + jnp.arange(span, dtype=jnp.int32)).astype(F32)
        frequency = jnp.exp(-jnp.log(150000.0) * jnp.arange(HALF, dtype=F32) / HALF)
        angle = frequency[:, None] * positions[None, :]
        turn = jnp.stack([jnp.cos(angle), jnp.sin(angle)])

        def rotated(vector, turn_ref, at):
            a, b = vector[:HALF], vector[HALF:]
            cosine, sine = turn_ref[0, :, at], turn_ref[1, :, at]
            return jnp.concatenate([a * cosine - b * sine, b * cosine + a * sine], axis=0)

        def lanes_of(index):
            return pl.ds(pl.multiple_of(index * block, LANES), block)

        early = n_group - 1
        sets = [(0, 1), tuple(range(2, inner))] if inner > 2 else [(0, 1)]

        def project(members):
            chosen = [entry for entry in blocks if entry[0] in members]
            n_parts = len(chosen)
            n_weights = n_group + 2 * early
            size = len(members) * block

            def body(at, where_ref, turn_ref, *refs):
                parts, refs = refs[:n_parts], refs[n_parts:]
                weight_refs, refs = refs[:n_weights], refs[n_weights:]
                kv_out, left_out, right_out, scale_out, late_out, x, kvs, full, sems = refs
                pairs = [(ref, kvs.at[s]) for s, ref in enumerate(weight_refs[:n_group])]
                for s in range(early):
                    for a in range(2):
                        lanes = pl.ds(a * half_cols, half_cols)
                        pairs.append((weight_refs[n_group + a * early + s], full.at[s, :, lanes]))
                for ref, (m, t, r, _) in zip(parts, chosen):
                    first_row = 0
                    if t is not None:
                        first_row = lax.rem(at[1] + split - t, split) * part + r
                        first_row = pl.multiple_of(first_row, 16)
                    lanes = pl.ds(members.index(m) * block, block)
                    pairs.append((ref, x.at[pl.ds(first_row, ref.shape[0]), lanes]))
                copies = fetch(pairs, sems)
                for copy in copies[:n_group]:
                    copy.wait()
                for s in range(n_group):
                    full[s, :, cols:] = jnp.zeros((deep, LANES), BF16)
                    full[s, :kv_deep, cols : cols + HEAD_DIM] = kvs[s, :, :HEAD_DIM]
                    full[s, kv_deep:, cols : cols + HEAD_DIM] = kvs[s, : deep - kv_deep, HEAD_DIM:]
                for copy in copies[n_group:n_weights]:
                    copy.wait()
                spots = [
                    pl.ds(pl.multiple_of(where_ref[s] * deep, 16), deep) for s in range(n_group)
                ]
                for j, m in enumerate(members):
                    for copy, entry in zip(copies[n_weights:], chosen):
                        if entry[0] == m:
                            copy.wait()
                    lanes = slice(j * block, (j + 1) * block)
                    late_out[:, lanes] = x[spots[early], lanes]
                    squares = jnp.zeros((1, block), F32)
                    for s in range(n_group):
                        piece = x[s * deep : (s + 1) * deep, lanes].astype(F32)
                        squares = squares + jnp.sum(piece * piece, axis=0, keepdims=True)
                    scale = lax.rsqrt(squares / width + 1e-05)
                    scale_out[:, lanes] = scale
                    total = contract(full[early, :, cols:], x[spots[early], lanes])[:HEAD_DIM]
                    begun = None
                    for s in range(early):
                        added = contract(full[s], x[spots[s], lanes])
                        total = total + added[cols : cols + HEAD_DIM]
                        begun = added[:cols] if begun is None else begun + added[:cols]
                    left_out[:, lanes] = begun[:half_cols]
                    right_out[:, lanes] = begun[half_cols:]
                    total = total * scale
                    turned = rotated(total, turn_ref, lanes_of(at[0] ^ m))
                    kv_out[:, lanes] = jnp.where(at[0] % 2 == 0, turned, total).astype(BF16)

            return call(
                body,
                [
                    jax.ShapeDtypeStruct((HEAD_DIM, size), BF16),
                    jax.ShapeDtypeStruct((half_cols, size), F32),
                    jax.ShapeDtypeStruct((half_cols, size), F32),
                    jax.ShapeDtypeStruct((1, size), F32),
                    jax.ShapeDtypeStruct((deep, size), BF16),
                ],
                (
                    place,
                    where,
                    turn,
                    *[x for _, _, _, x in chosen],
                    *kv_parts,
                    *left_parts[:early],
                    *right_parts[:early],
                ),
                [SMEM, SMEM, VMEM] + [HBM] * (n_parts + n_weights),
                scratch=[
                    pltpu.VMEM((width, size), BF16),
                    pltpu.VMEM((n_group, kv_deep, LANES), BF16),
                    pltpu.VMEM((n_group, deep, wide), BF16),
                    pltpu.SemaphoreType.DMA((n_parts + n_weights,)),
                ],
                flops=2 * width * (cols + HEAD_DIM) * size,
            )

        projected = [project(members) for members in sets]
        kv_sets = [p[0] for p in projected]
        if outer == 1:
            kv_pair = kv_sets + [swap(x, "role", n_role, 1) for x in kv_sets]
            flip = mine % 2
        else:
            natural = jnp.zeros((HEAD_DIM, span), BF16)
            for x, members in zip(kv_sets, sets):
                for j, m in enumerate(members):
                    piece = x[:, j * block : (j + 1) * block]
                    natural = lax.dynamic_update_slice(natural, piece, (0, (mine ^ m) * block))
            both = lax.all_gather(natural, "role", axis=0).reshape(outer, inner, HEAD_DIM, span)

            def along(index):
                taken = lax.dynamic_index_in_dim(both, index, 1, keepdims=False)
                return jnp.swapaxes(taken, 0, 1).reshape(HEAD_DIM, seq)

            kv_pair = [along((mine // 2) * 2), along((mine // 2) * 2 + 1)]
            flip = jnp.int32(0)

        gathered = [(0, segments)]
        bit = n_role // 2
        while bit:
            gathered += [(m ^ bit, swap(x, "role", n_role, bit)) for m, x in gathered]
            bit //= 2
        docs = jnp.zeros((n_role, block), jnp.int32)
        for m, x in gathered:
            docs = lax.dynamic_update_slice(docs, x, (role ^ m, 0))
        docs = docs.reshape(seq)
        own_docs = lax.dynamic_slice(docs, (ring * span,), (span,))
        first = jnp.sum((docs[:, None] < own_docs[None, :]).astype(jnp.int32), axis=0)[None, :]
        sink_terms = jnp.exp(sinks)
        turns = jnp.stack([mine, flip, ring]).astype(jnp.int32)

        copies_out = n_tensor if outer == 1 else 1
        n_sets = len(sets)
        n_kv = len(kv_pair)
        many = half_heads * block

        def finish(half):
            def body(at, sink_ref, first_ref, turn_ref, weight_ref, *refs):
                begun_refs, refs = refs[:n_sets], refs[n_sets:]
                scale_refs, refs = refs[:n_sets], refs[n_sets:]
                late_refs, refs = refs[:n_sets], refs[n_sets:]
                kv_refs, (out_ref, one_ref, two_ref, k_ref, v_ref, q_ref) = refs[:n_kv], refs[n_kv:]
                if outer == 1:
                    for i, members in enumerate(sets):
                        for j, m in enumerate(members):
                            lanes = slice(j * block, (j + 1) * block)
                            one_ref[:, lanes_of(at[0] ^ m)] = kv_refs[i][:, lanes]
                            two_ref[:, lanes_of(at[0] ^ 1 ^ m)] = kv_refs[n_sets + i][:, lanes]
                    one, two = one_ref[...], two_ref[...]
                    k_ref[...] = jnp.where(at[1] == 0, one, two)
                    v_ref[...] = jnp.where(at[1] == 0, two, one)
                else:
                    k_ref, v_ref = kv_refs
                for i, members in enumerate(sets):
                    for j, m in enumerate(members):
                        lanes = slice(j * block, (j + 1) * block)
                        spot = lanes_of(at[0] ^ m)
                        total = contract(weight_ref[...], late_refs[i][:, lanes])
                        total = total + begun_refs[i][:, lanes]
                        total = total * (scale_refs[i][:, lanes] * 0.125)
                        for h in range(half_heads):
                            here = slice(h * HEAD_DIM, (h + 1) * HEAD_DIM)
                            q_ref[here, spot] = rotated(total[here], turn_ref, spot).astype(BF16)
                for qb in range(inner):
                    lanes = slice(qb * block, (qb + 1) * block)
                    query = jnp.concatenate(
                        [
                            q_ref[h * HEAD_DIM : (h + 1) * HEAD_DIM, lanes]
                            for h in range(half_heads)
                        ],
                        axis=1,
                    )
                    start = jnp.concatenate([first_ref[:, lanes]] * half_heads, axis=1)
                    offset = qb * block + lax.broadcasted_iota(jnp.int32, (1, block), 1)
                    pos = at[2] * span + jnp.concatenate([offset] * half_heads, axis=1)

                    def terms(at_key, keys):
                        index = at_key + lax.broadcasted_iota(jnp.int32, (keys, many), 0)
                        allowed = (index >= start) & (index <= pos)
                        there = slice(0, keys) if outer == 1 else pl.ds(at_key, keys)
                        scores = contract(k_ref[:, there], query)
                        weight = jnp.where(allowed, jnp.exp(scores), 0.0)
                        total = jnp.sum(weight, axis=0, keepdims=True)
                        summed = jnp.dot(
                            v_ref[:, there], weight.astype(BF16), preferred_element_type=F32
                        )
                        return total, summed

                    def advance(i, carry):
                        added = terms(pl.multiple_of(i * span, LANES), span)
                        return carry[0] + added[0], carry[1] + added[1]

                    if outer == 1:
                        total, summed = terms(0, (qb + 1) * block)
                    else:
                        here = terms(pl.multiple_of(at[2] * span, LANES), (qb + 1) * block)
                        total, summed = lax.fori_loop(0, at[2], advance, here)
                    for h in range(half_heads):
                        lanes = slice(h * block, (h + 1) * block)
                        sink = sink_ref[at[0] * heads + half * half_heads + h]
                        value = (summed[:, lanes] / (total[:, lanes] + sink)).astype(BF16)
                        here = slice(h * HEAD_DIM, (h + 1) * HEAD_DIM)
                        for copy in range(copies_out):
                            out_ref[copy * inner + qb, here, :] = value

            weight = (left_parts, right_parts)[half][early]
            return call(
                body,
                jax.ShapeDtypeStruct((copies_out * inner, half_cols, block), BF16),
                (
                    turns,
                    sink_terms,
                    first,
                    turn,
                    weight,
                    *[p[1 + half] for p in projected],
                    *[p[3] for p in projected],
                    *[p[4] for p in projected],
                    *kv_pair,
                ),
                [SMEM, SMEM] + [VMEM] * (3 + 3 * n_sets + n_kv),
                scratch=[pltpu.VMEM((HEAD_DIM, span), BF16)] * 2
                + [pltpu.VMEM((HEAD_DIM, span), BF16)] * 2
                + [pltpu.VMEM((half_cols, span), BF16)],
                flops=half_heads * 4 * HEAD_DIM * span * seq // 2,
            )

        def exchange(context):
            if outer == 1:
                return lax.all_to_all(context, ("tensor", "role"), 0, 0, tiled=True)
            pieces_in = []
            for k in range(inner):
                piece = lax.dynamic_index_in_dim(context, mine ^ k, 0, keepdims=False)
                pieces_in.append(swap(piece, "role", n_role, k) if k else piece)
            stacked = jnp.stack(pieces_in)
            ordered = jnp.stack(
                [lax.dynamic_index_in_dim(stacked, mine ^ i, 0, keepdims=False) for i in range(inner)]
            )
            every = lax.all_gather(ordered, "tensor", axis=0)
            return every.reshape(n_tensor * inner, half_cols, block)

        halves = [finish(half) for half in range(2)]
        context = [exchange(half) for half in halves]

        shared = out_weight.T
        if last_token is not None:
            shared, _ = lax.optimization_barrier((shared, last_token))
        weights_out = [(0, shared)]
        bit = n_role // 2
        while bit:
            ready = [x for _, x in weights_out]
            if bit == 1:
                *ready, _ = lax.optimization_barrier((*ready, halves[0]))
            weights_out += [
                (m ^ bit, swap(x, "role", n_role, bit))
                for (m, _), x in zip(weights_out, ready)
            ]
            bit //= 2

        table = jnp.stack([role ^ m for m, _ in weights_out]).astype(jnp.int32)

        units = out_rows // (2 * half_cols)
        phased = units * 2 * half_cols == out_rows
        lists = [x for _, x in weights_out]

        def dots(table_ref, weight, source):
            total = None
            for k in range(n_role):
                added = jnp.dot(weight(k), source(table_ref[k]), preferred_element_type=F32)
                total = added if total is None else total + added
            return total

        def mix(half, begun_mix):
            def body(table_ref, context_ref, *refs):
                if half:
                    before, refs = refs[0], refs[1:]
                hbm, (out_ref, held_ref, sems) = refs[:n_role], refs[n_role:]
                pairs = []
                for k in range(n_role):
                    for u in range(units):
                        there = pl.ds((2 * u + half) * half_cols, half_cols)
                        here = pl.ds(u * half_cols, half_cols)
                        pairs.append((hbm[k].at[:, there], held_ref.at[k, :, here]))
                for copy in fetch(pairs, sems):
                    copy.wait()

                def source(b):
                    return context_ref[pl.ds(b * units, units)].reshape(units * half_cols, block)

                total = dots(table_ref, lambda k: held_ref[k], source)
                out_ref[...] = (total + before[...]).astype(BF16) if half else total

            return call(
                body,
                jax.ShapeDtypeStruct((out_cols, block), BF16 if half else F32),
                (table, context[half], *([begun_mix] if half else []), *lists),
                [SMEM, VMEM] + [VMEM] * half + [HBM] * n_role,
                scratch=[
                    pltpu.VMEM((n_role, out_cols, units * half_cols), BF16),
                    pltpu.SemaphoreType.DMA((n_role * units,)),
                ],
                flops=n_role * out_rows * out_cols * block,
            )

        def out_body(table_ref, one_ref, two_ref, *refs):
            weights, out_ref, nat = refs[:n_role], refs[n_role], refs[n_role + 1]
            for i in range(n_tensor * inner):
                nat[i * cols : i * cols + half_cols] = one_ref[i]
                nat[i * cols + half_cols : (i + 1) * cols] = two_ref[i]

            def source(b):
                return nat[pl.ds(pl.multiple_of(b * out_rows, 16), out_rows), :]

            total = dots(table_ref, lambda k: weights[k][...], source)
            out_ref[...] = total.astype(BF16)

        if phased:
            mixed = mix(1, mix(0, None))
        else:
            mixed = call(
                out_body,
                jax.ShapeDtypeStruct((out_cols, block), BF16),
                (table, *context, *lists),
                [SMEM] + [VMEM] * (2 + n_role),
                scratch=[pltpu.VMEM((n_role * out_rows, block), BF16)],
                flops=2 * n_role * out_rows * out_cols * block,
            )
        return mixed.T[None]

    return on_device


def solution(mesh):
    placed = (
        P("group", "role", None),
        P(),
        P(("group", "role"), "tensor"),
        P(("group", "role"), "tensor"),
        P("role", "tensor"),
        P("tensor"),
        P("group", "role"),
    )
    return jax.shard_map(
        make_step(mesh),
        mesh=mesh,
        in_specs=placed,
        out_specs=P("group", "role", "tensor"),
        check_vma=False,
    )
```

```python
import jax
import jax.numpy as jnp
from jax import lax
from jax.experimental import pallas as pl
from jax.experimental.pallas import tpu as pltpu
from jax.sharding import PartitionSpec as P


HEAD_DIM = 64
HALF = HEAD_DIM // 2
LANES = 128
BF16 = jnp.bfloat16
F32 = jnp.float32


VMEM = pl.BlockSpec(memory_space=pltpu.VMEM)
SMEM = pl.BlockSpec(memory_space=pltpu.SMEM)
HBM = pl.BlockSpec(memory_space=pltpu.HBM)


def call(body, outs, args, specs, scratch=(), flops=0, moved=0, limit=60, where=VMEM):
    return pl.pallas_call(
        body,
        out_shape=outs,
        in_specs=specs,
        out_specs=jax.tree.map(lambda _: where, outs),
        scratch_shapes=scratch,
        compiler_params=pltpu.CompilerParams(vmem_limit_bytes=limit << 20),
        cost_estimate=pl.CostEstimate(flops=flops, bytes_accessed=moved, transcendentals=0),
    )(*args)


def swap(array, axis, size, mask):
    return lax.ppermute(array, axis, [(i, i ^ mask) for i in range(size)])


def fetch(pairs, sems, order=None):
    copies = [pltpu.make_async_copy(a, b, sems.at[i]) for i, (a, b) in enumerate(pairs)]
    for i in order or range(len(copies)):
        copies[i].start()
    return copies


def contract(left, right):
    return lax.dot_general(left, right, (((0,), (0,)), ((), ())), preferred_element_type=F32)


def make_step(mesh):
    n_group, n_tensor, n_role = mesh.shape["group"], mesh.shape["tensor"], mesh.shape["role"]

    def on_device(tokens, gain, q_weight, kv_weight, out_weight, sinks, segments):
        block = tokens.shape[1]
        width = tokens.shape[2]
        rows, q_cols = q_weight.shape
        pair_cols = kv_weight.shape[1]
        pairs = pair_cols // (2 * HEAD_DIM)
        inner = 2 * pairs
        outer = n_role // inner
        cols = q_cols // inner
        heads = cols // HEAD_DIM
        half_cols = cols // 2
        half_heads = heads // 2
        span = inner * block
        seq = n_role * block
        out_rows, out_cols = out_weight.shape
        split = n_tensor if inner > 2 and width % (16 * n_tensor) == 0 else 1
        part = width // split

        group = lax.axis_index("group")
        plane = lax.axis_index("tensor")
        role = lax.axis_index("role")
        mine = role % inner
        ring = role // inner
        place = jnp.stack([mine, plane, ring]).astype(jnp.int32)

        wide = cols + LANES

        own = tokens[0].T
        chunks = 2 if split > 1 and part % 32 == 0 else split - 1
        chunk = part // max(chunks, 1)

        def pack_body(at, q_hbm, kv_hbm, x_hbm, *outs):
            outs, halves, (q_ref, kv_ref, sems) = (
                outs[:inner],
                outs[inner : inner + chunks],
                outs[inner + chunks :],
            )
            pairs = [(q_hbm, q_ref), (kv_hbm, kv_ref)]
            for i, half_ref in enumerate(halves):
                first_row = pl.multiple_of(at[1] * part + i * chunk, 16)
                pairs.append((x_hbm.at[pl.ds(first_row, chunk)], half_ref))
            copies = fetch(pairs, sems)
            for copy in copies[:2]:
                copy.wait()
            for k in range(inner):
                target = at[0] ^ k
                outs[k][:, :cols] = q_ref[:, pl.ds(pl.multiple_of(target * cols, LANES), cols)]
                pair = kv_ref[:, pl.ds(pl.multiple_of((target // 2) * LANES, LANES), LANES)]
                chosen = jnp.where(target % 2 == 0, pair[:, :HEAD_DIM], pair[:, HEAD_DIM:])
                outs[k][:, cols : cols + HEAD_DIM] = chosen
                outs[k][:, cols + HEAD_DIM :] = jnp.zeros((rows, HEAD_DIM), BF16)
            for copy in copies[2:]:
                copy.wait()

        packed = call(
            pack_body,
            [jax.ShapeDtypeStruct((rows, wide), BF16)] * inner
            + [jax.ShapeDtypeStruct((chunk, block), BF16)] * chunks,
            (place, q_weight, kv_weight, own),
            [SMEM, HBM, HBM, HBM],
            scratch=[
                pltpu.VMEM(q_weight.shape, BF16),
                pltpu.VMEM(kv_weight.shape, BF16),
                pltpu.SemaphoreType.DMA((2 + chunks,)),
            ],
        )
        deep = n_role * rows
        kv_deep = -(-deep // 32) * 16

        def stacked(got, source_group):
            sources = [(0, k, x) for k, x in enumerate(got)]
            for o in range(1, outer):
                ahead = [(i, (i + o * inner) % n_role) for i in range(n_role)]
                sources += [(o, k, lax.ppermute(x, "role", ahead)) for k, x in enumerate(got)]
            rows_gain = lax.dynamic_slice(gain, (source_group * deep,), (deep,))
            rows_gain = jnp.broadcast_to(rows_gain[:, None], (deep, LANES))

            def stack_body(at, gain_ref, *refs):
                kv_out, left_out, right_out, one, two = refs[n_role:]
                for ref, (o, k, _) in zip(refs[:n_role], sources):
                    spot = lax.rem(at[2] + outer - o, outer) * inner + (at[0] ^ k)
                    one[spot] = ref[...]
                for p in range(n_role):
                    two[p * rows : (p + 1) * rows, :] = one[p].astype(F32)
                for out_ref, c in ((left_out, 0), (right_out, half_cols)):
                    for lane in range(0, half_cols, LANES):
                        here = slice(lane, lane + LANES)
                        there = slice(c + lane, c + lane + LANES)
                        out_ref[:, here] = (two[:, there] * gain_ref[...]).astype(BF16)
                kv = (two[:, cols:] * gain_ref[...])[:, :HEAD_DIM].astype(BF16)
                kv_out[...] = jnp.zeros_like(kv_out)
                kv_out[:, :HEAD_DIM] = kv[:kv_deep]
                kv_out[: deep - kv_deep, HEAD_DIM:] = kv[kv_deep:]

            return call(
                stack_body,
                [
                    jax.ShapeDtypeStruct((kv_deep, LANES), BF16),
                    jax.ShapeDtypeStruct((deep, half_cols), BF16),
                    jax.ShapeDtypeStruct((deep, half_cols), BF16),
                ],
                (place, rows_gain, *[x for _, _, x in sources]),
                [SMEM, VMEM] + [VMEM] * n_role,
                scratch=[
                    pltpu.VMEM((n_role, rows, wide), BF16),
                    pltpu.VMEM((deep, wide), F32),
                ],
                limit=8,
            )

        forward = [(i, (i + 1) % n_group) for i in range(n_group)]
        neighbours = []
        for k in range(inner):
            pairs = [
                (g * n_role + r, (g + 1) % n_group * n_role + (r ^ k))
                for g in range(n_group)
                for r in range(n_role)
            ]
            neighbours.append(lax.ppermute(packed[k], ("group", "role"), pairs))
        direct = stacked(neighbours, (group - 1) % n_group)
        near = [packed[0]] + [swap(packed[k], "role", n_role, k) for k in range(1, inner)]
        held = stacked(near, group)
        rings = [[x, y] for x, y in zip(held, direct)]
        for _ in range(2, n_group):
            for array in rings:
                array.append(lax.ppermute(array[-1], "group", forward))
        kv_parts, left_parts, right_parts = [array[:n_group] for array in rings]
        where = jnp.stack([(group - s) % n_group for s in range(n_group)]).astype(jnp.int32)

        blocks = [(0, None, 0, own)]
        bit = inner // 2
        last_token = None
        while bit:
            if bit > 1 and split > 1 and len(blocks) == 1:
                after = [(i, (i + 1) % split) for i in range(split)]
                for i in range(chunks):
                    piece = swap(packed[inner + i], "role", n_role, bit)
                    last_token = piece
                    blocks.append((bit, 0, i * chunk, piece))
                    for t in range(1, split):
                        piece = lax.ppermute(piece, "tensor", after)
                        blocks.append((bit, t, i * chunk, piece))
            else:
                blocks += [
                    (
                        m ^ bit,
                        t,
                        r,
                        swap(x, "role", n_role, bit),
                    )
                    for m, t, r, x in blocks
                ]
            bit //= 2

        positions = (ring * span + jnp.arange(span, dtype=jnp.int32)).astype(F32)
        frequency = jnp.exp(-jnp.log(150000.0) * jnp.arange(HALF, dtype=F32) / HALF)
        angle = frequency[:, None] * positions[None, :]
        turn = jnp.stack([jnp.cos(angle), jnp.sin(angle)])

        def rotated(vector, turn_ref, at):
            a, b = vector[:HALF], vector[HALF:]
            cosine, sine = turn_ref[0, :, at], turn_ref[1, :, at]
            return jnp.concatenate([a * cosine - b * sine, b * cosine + a * sine], axis=0)

        def lanes_of(index):
            return pl.ds(pl.multiple_of(index * block, LANES), block)

        early = n_group - 1
        sets = [(0, 1), tuple(range(2, inner))] if inner > 2 else [(0, 1)]

        def project(members):
            chosen = [entry for entry in blocks if entry[0] in members]
            n_parts = len(chosen)
            n_weights = n_group + 2 * early
            size = len(members) * block

            def body(at, where_ref, turn_ref, *refs):
                parts, refs = refs[:n_parts], refs[n_parts:]
                weight_refs, refs = refs[:n_weights], refs[n_weights:]
                kv_out, left_out, right_out, scale_out, late_out, x, kvs, full, sems = refs
                pairs = [(ref, kvs.at[s]) for s, ref in enumerate(weight_refs[:n_group])]
                for s in range(early):
                    for a in range(2):
                        lanes = pl.ds(a * half_cols, half_cols)
                        pairs.append((weight_refs[n_group + a * early + s], full.at[s, :, lanes]))
                for ref, (m, t, r, _) in zip(parts, chosen):
                    first_row = 0
                    if t is not None:
                        first_row = lax.rem(at[1] + split - t, split) * part + r
                        first_row = pl.multiple_of(first_row, 16)
                    lanes = pl.ds(members.index(m) * block, block)
                    pairs.append((ref, x.at[pl.ds(first_row, ref.shape[0]), lanes]))
                first_set = [
                    n_weights + i for i, entry in enumerate(chosen) if entry[0] == members[0]
                ]
                order = list(range(n_group)) + first_set
                order += [i for i in range(n_group, len(pairs)) if i not in first_set]
                copies = fetch(pairs, sems, order)
                for copy in copies[:n_group]:
                    copy.wait()
                for s in range(n_group):
                    full[s, :, cols:] = jnp.zeros((deep, LANES), BF16)
                    full[s, :kv_deep, cols : cols + HEAD_DIM] = kvs[s, :, :HEAD_DIM]
                    full[s, kv_deep:, cols : cols + HEAD_DIM] = kvs[s, : deep - kv_deep, HEAD_DIM:]
                spots = [
                    pl.ds(pl.multiple_of(where_ref[s] * deep, 16), deep) for s in range(n_group)
                ]
                for j, m in enumerate(members):
                    for copy, entry in zip(copies[n_weights:], chosen):
                        if entry[0] == m:
                            copy.wait()
                    lanes = slice(j * block, (j + 1) * block)
                    late_out[:, lanes] = x[spots[early], lanes]
                    squares = jnp.zeros((1, block), F32)
                    for s in range(n_group):
                        piece = x[s * deep : (s + 1) * deep, lanes].astype(F32)
                        squares = squares + jnp.sum(piece * piece, axis=0, keepdims=True)
                    scale = lax.rsqrt(squares / width + 1e-05)
                    scale_out[:, lanes] = scale
                    total = contract(full[early, :, cols:], x[spots[early], lanes])[:HEAD_DIM]
                    begun = None
                    for s in range(early):
                        if j == 0:
                            for copy in copies[n_group + 2 * s : n_group + 2 * s + 2]:
                                copy.wait()
                        added = contract(full[s], x[spots[s], lanes])
                        total = total + added[cols : cols + HEAD_DIM]
                        begun = added[:cols] if begun is None else begun + added[:cols]
                    left_out[:, lanes] = begun[:half_cols]
                    right_out[:, lanes] = begun[half_cols:]
                    total = total * scale
                    turned = rotated(total, turn_ref, lanes_of(at[0] ^ m))
                    kv_out[:, lanes] = jnp.where(at[0] % 2 == 0, turned, total).astype(BF16)

            return call(
                body,
                [
                    jax.ShapeDtypeStruct((HEAD_DIM, size), BF16),
                    jax.ShapeDtypeStruct((half_cols, size), F32),
                    jax.ShapeDtypeStruct((half_cols, size), F32),
                    jax.ShapeDtypeStruct((1, size), F32),
                    jax.ShapeDtypeStruct((deep, size), BF16),
                ],
                (
                    place,
                    where,
                    turn,
                    *[x for _, _, _, x in chosen],
                    *kv_parts,
                    *left_parts[:early],
                    *right_parts[:early],
                ),
                [SMEM, SMEM, VMEM] + [HBM] * (n_parts + n_weights),
                scratch=[
                    pltpu.VMEM((width, size), BF16),
                    pltpu.VMEM((n_group, kv_deep, LANES), BF16),
                    pltpu.VMEM((n_group, deep, wide), BF16),
                    pltpu.SemaphoreType.DMA((n_parts + n_weights,)),
                ],
                flops=2 * width * (cols + HEAD_DIM) * size,
            )

        projected = [project(members) for members in sets]
        kv_sets = [p[0] for p in projected]
        if outer == 1:
            kv_pair = kv_sets + [swap(x, "role", n_role, 1) for x in kv_sets]
            flip = mine % 2
        else:
            natural = jnp.zeros((HEAD_DIM, span), BF16)
            for x, members in zip(kv_sets, sets):
                for j, m in enumerate(members):
                    piece = x[:, j * block : (j + 1) * block]
                    natural = lax.dynamic_update_slice(natural, piece, (0, (mine ^ m) * block))
            both = lax.all_gather(natural, "role", axis=0).reshape(outer, inner, HEAD_DIM, span)

            def along(index):
                taken = lax.dynamic_index_in_dim(both, index, 1, keepdims=False)
                return jnp.swapaxes(taken, 0, 1).reshape(HEAD_DIM, seq)

            kv_pair = [along((mine // 2) * 2), along((mine // 2) * 2 + 1)]
            flip = jnp.int32(0)

        gathered = [(0, segments)]
        bit = n_role // 2
        while bit:
            gathered += [(m ^ bit, swap(x, "role", n_role, bit)) for m, x in gathered]
            bit //= 2
        docs = jnp.zeros((n_role, block), jnp.int32)
        for m, x in gathered:
            docs = lax.dynamic_update_slice(docs, x, (role ^ m, 0))
        docs = docs.reshape(seq)
        own_docs = lax.dynamic_slice(docs, (ring * span,), (span,))
        first = jnp.sum((docs[:, None] < own_docs[None, :]).astype(jnp.int32), axis=0)[None, :]
        sink_terms = jnp.exp(sinks)
        turns = jnp.stack([mine, flip, ring]).astype(jnp.int32)

        copies_out = n_tensor if outer == 1 else 1
        n_sets = len(sets)
        n_kv = len(kv_pair)
        many = half_heads * block

        def finish(half):
            def body(at, sink_ref, first_ref, turn_ref, weight_ref, *refs):
                begun_refs, refs = refs[:n_sets], refs[n_sets:]
                scale_refs, refs = refs[:n_sets], refs[n_sets:]
                late_refs, refs = refs[:n_sets], refs[n_sets:]
                kv_refs, (out_ref, one_ref, two_ref, k_ref, v_ref, q_ref) = refs[:n_kv], refs[n_kv:]
                if outer == 1:
                    for i, members in enumerate(sets):
                        for j, m in enumerate(members):
                            lanes = slice(j * block, (j + 1) * block)
                            one_ref[:, lanes_of(at[0] ^ m)] = kv_refs[i][:, lanes]
                            two_ref[:, lanes_of(at[0] ^ 1 ^ m)] = kv_refs[n_sets + i][:, lanes]
                    one, two = one_ref[...], two_ref[...]
                    k_ref[...] = jnp.where(at[1] == 0, one, two)
                    v_ref[...] = jnp.where(at[1] == 0, two, one)
                else:
                    k_ref, v_ref = kv_refs
                for i, members in enumerate(sets):
                    for j, m in enumerate(members):
                        lanes = slice(j * block, (j + 1) * block)
                        spot = lanes_of(at[0] ^ m)
                        total = contract(weight_ref[...], late_refs[i][:, lanes])
                        total = total + begun_refs[i][:, lanes]
                        total = total * (scale_refs[i][:, lanes] * 0.125)
                        for h in range(half_heads):
                            here = slice(h * HEAD_DIM, (h + 1) * HEAD_DIM)
                            q_ref[here, spot] = rotated(total[here], turn_ref, spot).astype(BF16)
                for qb in range(inner):
                    lanes = slice(qb * block, (qb + 1) * block)
                    query = jnp.concatenate(
                        [
                            q_ref[h * HEAD_DIM : (h + 1) * HEAD_DIM, lanes]
                            for h in range(half_heads)
                        ],
                        axis=1,
                    )
                    start = jnp.concatenate([first_ref[:, lanes]] * half_heads, axis=1)
                    offset = qb * block + lax.broadcasted_iota(jnp.int32, (1, block), 1)
                    pos = at[2] * span + jnp.concatenate([offset] * half_heads, axis=1)

                    def terms(at_key, keys):
                        index = at_key + lax.broadcasted_iota(jnp.int32, (keys, many), 0)
                        allowed = (index >= start) & (index <= pos)
                        there = slice(0, keys) if outer == 1 else pl.ds(at_key, keys)
                        scores = contract(k_ref[:, there], query)
                        weight = jnp.where(allowed, jnp.exp(scores), 0.0)
                        total = jnp.sum(weight, axis=0, keepdims=True)
                        summed = jnp.dot(
                            v_ref[:, there], weight.astype(BF16), preferred_element_type=F32
                        )
                        return total, summed

                    def advance(i, carry):
                        added = terms(pl.multiple_of(i * span, LANES), span)
                        return carry[0] + added[0], carry[1] + added[1]

                    if outer == 1:
                        total, summed = terms(0, (qb + 1) * block)
                    else:
                        here = terms(pl.multiple_of(at[2] * span, LANES), (qb + 1) * block)
                        total, summed = lax.fori_loop(0, at[2], advance, here)
                    for h in range(half_heads):
                        lanes = slice(h * block, (h + 1) * block)
                        sink = sink_ref[at[0] * heads + half * half_heads + h]
                        value = (summed[:, lanes] / (total[:, lanes] + sink)).astype(BF16)
                        here = slice(h * HEAD_DIM, (h + 1) * HEAD_DIM)
                        for copy in range(copies_out):
                            out_ref[copy * inner + qb, here, :] = value

            weight = (left_parts, right_parts)[half][early]
            return call(
                body,
                jax.ShapeDtypeStruct((copies_out * inner, half_cols, block), BF16),
                (
                    turns,
                    sink_terms,
                    first,
                    turn,
                    weight,
                    *[p[1 + half] for p in projected],
                    *[p[3] for p in projected],
                    *[p[4] for p in projected],
                    *kv_pair,
                ),
                [SMEM, SMEM] + [VMEM] * (3 + 3 * n_sets + n_kv),
                scratch=[pltpu.VMEM((HEAD_DIM, span), BF16)] * 2
                + [pltpu.VMEM((HEAD_DIM, span), BF16)] * 2
                + [pltpu.VMEM((half_cols, span), BF16)],
                flops=half_heads * 4 * HEAD_DIM * span * seq // 2,
            )

        def exchange(context):
            if outer == 1:
                return lax.all_to_all(context, ("tensor", "role"), 0, 0, tiled=True)
            pieces_in = []
            for k in range(inner):
                piece = lax.dynamic_index_in_dim(context, mine ^ k, 0, keepdims=False)
                pieces_in.append(swap(piece, "role", n_role, k) if k else piece)
            stacked = jnp.stack(pieces_in)
            ordered = jnp.stack(
                [lax.dynamic_index_in_dim(stacked, mine ^ i, 0, keepdims=False) for i in range(inner)]
            )
            every = lax.all_gather(ordered, "tensor", axis=0)
            return every.reshape(n_tensor * inner, half_cols, block)

        halves = [finish(half) for half in range(2)]
        context = [exchange(half) for half in halves]

        shared = out_weight.T
        if last_token is not None:
            shared, _ = lax.optimization_barrier((shared, last_token))
        weights_out = [(0, shared)]
        bit = n_role // 2
        while bit:
            ready = [x for _, x in weights_out]
            if bit == 1:
                *ready, _ = lax.optimization_barrier((*ready, halves[0]))
            weights_out += [
                (m ^ bit, swap(x, "role", n_role, bit))
                for (m, _), x in zip(weights_out, ready)
            ]
            bit //= 2

        table = jnp.stack([role ^ m for m, _ in weights_out]).astype(jnp.int32)

        units = out_rows // (2 * half_cols)
        phased = units * 2 * half_cols == out_rows
        lists = [x for _, x in weights_out]

        def dots(table_ref, weight, source):
            total = None
            for k in range(n_role):
                added = jnp.dot(weight(k), source(table_ref[k]), preferred_element_type=F32)
                total = added if total is None else total + added
            return total

        bands = 5 if out_cols % (5 * 16) == 0 else 1
        band = out_cols // bands

        def mix(half, begun_mix):
            def body(table_ref, context_ref, *refs):
                if half:
                    before, refs = refs[0], refs[1:]
                hbm, refs = refs[:n_role], refs[n_role:]
                out_hbm, held_ref, made_ref, sems = refs[:4]
                pairs = []
                for i in range(bands):
                    across = pl.ds(i * band, band)
                    for k in range(n_role):
                        for u in range(units):
                            there = pl.ds((2 * u + half) * half_cols, half_cols)
                            here = pl.ds(u * half_cols, half_cols)
                            pairs.append(
                                (hbm[k].at[across, there], held_ref.at[k, across, here])
                            )
                    if half:
                        pairs.append((before.at[across], refs[4].at[across]))
                copies = fetch(pairs, sems)
                each = len(pairs) // bands

                def source(b):
                    return context_ref[pl.ds(b * units, units)].reshape(units * half_cols, block)

                done = []
                for i in range(bands):
                    for copy in copies[i * each : (i + 1) * each]:
                        copy.wait()
                    across = slice(i * band, (i + 1) * band)
                    total = dots(table_ref, lambda k: held_ref[k, across, :], source)
                    if half:
                        total = total + refs[4][across, :]
                    made_ref[across, :] = total.astype(made_ref.dtype)
                    here = pl.ds(i * band, band)
                    done.append(
                        pltpu.make_async_copy(
                            made_ref.at[here], out_hbm.at[here], sems.at[len(pairs) + i]
                        )
                    )
                    done[-1].start()
                for copy in done:
                    copy.wait()

            kind = BF16 if half else F32
            return call(
                body,
                jax.ShapeDtypeStruct((out_cols, block), kind),
                (table, context[half], *([begun_mix] if half else []), *lists),
                [SMEM, VMEM] + [HBM] * (half + n_role),
                scratch=[
                    pltpu.VMEM((n_role, out_cols, units * half_cols), BF16),
                    pltpu.VMEM((out_cols, block), kind),
                    pltpu.SemaphoreType.DMA((bands * (n_role * units + half + 1),)),
                ]
                + [pltpu.VMEM((out_cols, block), F32)] * half,
                flops=n_role * out_rows * out_cols * block,
                where=HBM,
            )

        def out_body(table_ref, one_ref, two_ref, *refs):
            weights, out_ref, nat = refs[:n_role], refs[n_role], refs[n_role + 1]
            for i in range(n_tensor * inner):
                nat[i * cols : i * cols + half_cols] = one_ref[i]
                nat[i * cols + half_cols : (i + 1) * cols] = two_ref[i]

            def source(b):
                return nat[pl.ds(pl.multiple_of(b * out_rows, 16), out_rows), :]

            total = dots(table_ref, lambda k: weights[k][...], source)
            out_ref[...] = total.astype(BF16)

        if phased:
            mixed = mix(1, mix(0, None))
        else:
            mixed = call(
                out_body,
                jax.ShapeDtypeStruct((out_cols, block), BF16),
                (table, *context, *lists),
                [SMEM] + [VMEM] * (2 + n_role),
                scratch=[pltpu.VMEM((n_role * out_rows, block), BF16)],
                flops=2 * n_role * out_rows * out_cols * block,
            )
        return mixed.T[None]

    return on_device


def solution(mesh):
    placed = (
        P("group", "role", None),
        P(),
        P(("group", "role"), "tensor"),
        P(("group", "role"), "tensor"),
        P("role", "tensor"),
        P("tensor"),
        P("group", "role"),
    )
    return jax.shard_map(
        make_step(mesh),
        mesh=mesh,
        in_specs=placed,
        out_specs=P("group", "role", "tensor"),
        check_vma=False,
    )
```
